128 devices in a mesh: req: 32 (over x, y, core), tp: 4 (over z).
Axes of the slice: x: 4, y: 4, z: 4, core: 2. Of those that a mesh axis runs over, the one named last changes fastest.
Arguments:
- hidden_in: bfloat16 [32768, 2048], P('req'), may hold values from -6 to 6
- norm_gain: bfloat16 [2048], replicated, may hold values from 0.099609375 to 1.8984375
- w_query: bfloat16 [2048, 1280], P(None, 'tp'), may hold values from -0.125 to 0.125
- key_value_weight: bfloat16 [2048, 640], replicated, may hold values from -0.3125 to 0.3125
- w_out: bfloat16 [1280, 2048], replicated, may hold values from -0.625 to 0.625
- prior_cache: bfloat16 [32, 7168, 640], P('req'), may hold values from -52 to 52
- cache_len: int32 [32], P('req'), may hold values from 1 to 7168, 114688 in all
- group_len: int32 [32], P('req'), may hold values from 1 to 1024, 16384 in all
- page_map: int32 [32, 128], P('req'), may hold values from 0 to 127, each once within a row
Outputs:
- hidden_out: bfloat16 [32768, 2048], P(('req', 'tp'))
- decode_kv: bfloat16 [128, 32, 64, 640], P(('req', 'tp'))
The draws below stay inside these ranges and needn't reach their ends.
Inputs may be any that keep to these rules, and one draw needn't show every extreme that they name: `page_map`: each row names every device index once.
All inputs are finite; a program needn't handle non-finite values. No bound on the sum of `cache_len` or of `group_len` on one device may be relied on, other than what follows from the above.
Results may differ from the reference program's by a relative error of at most 0.014.
The reference program's roundings to bfloat16 on the way count: a program that leaves them out, or rounds other values in their place, can miss the bound.
Values may be sent and summed in bfloat16 or wider, within the bound.
No kernel may reach another device: no remote copies, remote signals or barrier semaphores. Data moves between devices by JAX's collectives and lax.ppermute only.
A program may use at most 128 MiB of HBM per device.

```python
import math
import jax
import jax.numpy as jnp
import numpy as np
from jax import lax

MODEL_WIDTH = 2048
QUERY_HEAD_COUNT = 20
KEY_VALUE_HEADS = 5
HEAD_SIZE = 64
NEW_TOKEN_SLOTS = 1024
PRIOR_SLOTS = 7168
KEYS_PER_BLOCK = 512
REQUEST_TOTAL = 32
TOKENS = 32768
N_REQ = 32
N_TP = 4
DEVICES = 128


def draw_prior_cache(key, part):
    array_shape = (REQUEST_TOTAL, PRIOR_SLOTS, 2 * KEY_VALUE_HEADS * HEAD_SIZE)
    first_key = jax.random.fold_in(key, 11)
    values = jnp.clip(2.5 * jax.random.normal(first_key, array_shape, jnp.float32), -10.0, 10.0)
    return values.astype(jnp.bfloat16)


def levels(own_key, dims, split, least, largest):
    level, own = 1.0, jax.random.fold_in(own_key, 6)
    for axis_at, blocks in split:
        steps = jnp.exp(jax.random.uniform(jax.random.fold_in(own, axis_at), (blocks,), jnp.float32, least / len(split), largest / len(split)))
        level = level * jnp.repeat(steps, dims[axis_at] // blocks).reshape([-1 if axis == axis_at else 1 for axis in range(len(dims))])
    return level


def split_up(number_of, total, most, skew):
    weights = [(1 << 20) // math.isqrt(rank ** skew) + 1 for rank in range(2, number_of + 1)]
    spare, counts = total - most - (number_of - 1), [1] * (number_of - 1)
    while spare > 0:
        candidates = [i for i in range(number_of - 1) if counts[i] < most]
        pool, remaining = sum([weights[i] for i in candidates]), spare
        for i in candidates:
            more = min(most - counts[i], max(1, remaining * weights[i] // pool), spare)
            counts[i] = counts[i] + more
            spare = spare - more
    return np.array([most] + counts)


def uneven(own_key, count, total, most, slope):
    if count == 2:
        one = jax.random.randint(own_key, (), max(1, total - most), min(most, total - 1) + 1)
        return jnp.stack([one, total - one])
    tallies = jnp.asarray(split_up(count, total, most, slope), jnp.int32)
    couples = (count - 1) // 2
    giver, sink = tallies[1:1 + 2 * couples:2], tallies[2:2 + 2 * couples:2]
    margin = jnp.minimum(giver - 1, most - sink)
    shifted = jax.random.randint(jax.random.fold_in(own_key, 1), (couples,), 0, 1 << 20) % (margin + 1)
    tallies = tallies.at[1:1 + 2 * couples:2].set(giver - shifted).at[2:2 + 2 * couples:2].set(sink + shifted)
    return tallies[jax.random.permutation(jax.random.fold_in(own_key, 2), count)]


def bell_draw(key, extent, width, reach, split=(), kind=jnp.bfloat16):
    gain = levels(key, extent, split, -0.22, 0.18) if split else 1.0
    array = jax.random.normal(key, extent, jnp.float32) * width * gain
    return jnp.minimum(jnp.maximum(array, -reach), reach).astype(kind)


def setup_inputs(seed: int = 0) -> dict:
    seeds = jax.random.split(jax.random.key(seed), 10)
    hidden_in = bell_draw(seeds[0], (TOKENS, MODEL_WIDTH), 1.0, 6.0, ((0, 32),))
    norm_gain = jnp.clip(1.0 + 0.18 * jax.random.normal(seeds[1], (MODEL_WIDTH,), jnp.float32), 0.099609375, 1.8984375).astype(jnp.bfloat16)
    w_query = bell_draw(seeds[2], (MODEL_WIDTH, QUERY_HEAD_COUNT * HEAD_SIZE), MODEL_WIDTH ** -0.5, 0.125, ((1, 4),))
    key_value_weight = bell_draw(seeds[3], (MODEL_WIDTH, 2 * KEY_VALUE_HEADS * HEAD_SIZE), (MODEL_WIDTH // 6) ** -0.5, 0.3125)
    w_out = bell_draw(seeds[4], (QUERY_HEAD_COUNT * HEAD_SIZE, MODEL_WIDTH), (QUERY_HEAD_COUNT * HEAD_SIZE // 16) ** -0.5, 0.625)
    prior_cache = draw_prior_cache(jax.random.fold_in(seeds[9], 71), 0)
    cache_len = uneven(seeds[6], REQUEST_TOTAL, REQUEST_TOTAL * PRIOR_SLOTS // 2, PRIOR_SLOTS, 2).astype(jnp.int32)
    group_len = uneven(seeds[7], REQUEST_TOTAL, REQUEST_TOTAL * NEW_TOKEN_SLOTS // 2, NEW_TOKEN_SLOTS, 2).astype(jnp.int32)
    page_map = jax.vmap(lambda own: jax.random.permutation(own, DEVICES))(jax.random.split(seeds[8], REQUEST_TOTAL)).reshape((REQUEST_TOTAL, DEVICES)).astype(jnp.int32)
    return dict(hidden_in=hidden_in, norm_gain=norm_gain, w_query=w_query, key_value_weight=key_value_weight, w_out=w_out, prior_cache=prior_cache, cache_len=cache_len, group_len=group_len, page_map=page_map)


def rotation_table(values, token_positions, heads):
    half_size = HEAD_SIZE // 2
    frequency = 10000.0 ** (-(jnp.arange(half_size, dtype=jnp.float32) * 2.0 / HEAD_SIZE))
    angles = token_positions.astype(jnp.float32)[:, None] * frequency[None, :]
    cosine = jnp.cos(angles)[:, None, :]
    sine_part = jnp.sin(angles)[:, None, :]
    shaped = values.reshape(values.shape[0], heads, HEAD_SIZE)
    first_half = shaped[..., :half_size]
    second_half = shaped[..., half_size:]
    turned = jnp.concatenate([first_half * cosine - second_half * sine_part, second_half * cosine + first_half * sine_part], axis=-1)
    return turned.reshape(values.shape)

def flash_step(carry, start, queries, every_key, every_value, cached, fresh, row_ids):
    top_score, denom_sum, weighted = carry
    key_tile = lax.dynamic_slice_in_dim(every_key, start, KEYS_PER_BLOCK, 0).astype(jnp.float32)
    value_tile = lax.dynamic_slice_in_dim(every_value, start, KEYS_PER_BLOCK, 0).astype(jnp.float32)
    columns = start + jnp.arange(KEYS_PER_BLOCK, dtype=jnp.int32)
    later = columns[None, :] - PRIOR_SLOTS
    allowed = (columns[None, :] < cached) | (later >= 0) & (later <= row_ids[:, None]) & (later < fresh)
    scores = jnp.einsum('qhd,khd->qhk', queries, key_tile) * HEAD_SIZE ** (-0.5)
    scores = jnp.where(allowed[:, None, :], scores, -1e+30)
    new_top = jnp.maximum(top_score, lax.optimization_barrier(jnp.max(scores, axis=-1)))
    rescale = jnp.exp(top_score - new_top)
    chances = jnp.where(allowed[:, None, :], jnp.exp(scores - new_top[..., None]), 0.0).astype(jnp.bfloat16)
    chances_wide = lax.optimization_barrier(chances).astype(jnp.float32)
    denom_sum = denom_sum * rescale + lax.optimization_barrier(jnp.sum(chances_wide, axis=-1))
    weighted = weighted * rescale[..., None] + jnp.einsum('qhk,khd->qhd', chances_wide, value_tile)
    return (new_top, denom_sum, weighted)

def reference(hidden_in, norm_gain, w_query, key_value_weight, w_out, prior_cache, cache_len, group_len, page_map):
    key_span_width = KEY_VALUE_HEADS * HEAD_SIZE
    device_count = N_REQ * N_TP
    block_rows = (PRIOR_SLOTS + NEW_TOKEN_SLOTS) // device_count

    def one_request(items):
        tokens, cache_rows, cached, fresh, mapping = items
        hidden = tokens.astype(jnp.float32)
        normed = (hidden * lax.rsqrt(lax.optimization_barrier(jnp.mean(hidden * hidden, axis=-1, keepdims=True)) + 1e-05) * norm_gain.astype(jnp.float32)).astype(jnp.bfloat16)
        row_ids = jnp.arange(NEW_TOKEN_SLOTS, dtype=jnp.int32)
        token_positions = cached + row_ids
        queries = rotation_table(jnp.dot(normed, w_query, preferred_element_type=jnp.float32), token_positions, QUERY_HEAD_COUNT).astype(jnp.bfloat16)
        unrotated_input = jnp.dot(normed, key_value_weight, preferred_element_type=jnp.float32)
        key_value_rows = jnp.concatenate([rotation_table(unrotated_input[:, :key_span_width], token_positions, KEY_VALUE_HEADS), unrotated_input[:, key_span_width:]], axis=1).astype(jnp.bfloat16)
        zero = jnp.zeros((), jnp.bfloat16)
        old_part = jnp.where((jnp.arange(PRIOR_SLOTS, dtype=jnp.int32) < cached)[:, None], cache_rows, zero)
        new_part = jnp.where((row_ids < fresh)[:, None], key_value_rows, zero)
        context_output = jnp.concatenate([old_part, new_part], axis=0)
        every_key = jnp.repeat(context_output[:, :key_span_width].reshape(PRIOR_SLOTS + NEW_TOKEN_SLOTS, KEY_VALUE_HEADS, HEAD_SIZE), QUERY_HEAD_COUNT // KEY_VALUE_HEADS, axis=1)
        every_value = jnp.repeat(context_output[:, key_span_width:].reshape(PRIOR_SLOTS + NEW_TOKEN_SLOTS, KEY_VALUE_HEADS, HEAD_SIZE), QUERY_HEAD_COUNT // KEY_VALUE_HEADS, axis=1)
        query_heads = queries.reshape(NEW_TOKEN_SLOTS, QUERY_HEAD_COUNT, HEAD_SIZE).astype(jnp.float32)
        initial = (jnp.full((NEW_TOKEN_SLOTS, QUERY_HEAD_COUNT), -1e+30, jnp.float32), jnp.zeros((NEW_TOKEN_SLOTS, QUERY_HEAD_COUNT), jnp.float32), jnp.zeros((NEW_TOKEN_SLOTS, QUERY_HEAD_COUNT, HEAD_SIZE), jnp.float32))

        def scan_step(carry, start):
            return (flash_step(carry, start, query_heads, every_key, every_value, cached, fresh, row_ids), None)
        starts = jnp.arange((PRIOR_SLOTS + NEW_TOKEN_SLOTS) // KEYS_PER_BLOCK, dtype=jnp.int32) * KEYS_PER_BLOCK
        final, unused = lax.scan(scan_step, initial, starts)
        heads_out = (final[2] / final[1][..., None]).astype(jnp.bfloat16).reshape(NEW_TOKEN_SLOTS, QUERY_HEAD_COUNT * HEAD_SIZE)
        mixed = jnp.dot(heads_out, w_out, preferred_element_type=jnp.float32)
        result = jnp.where((row_ids < fresh)[:, None], hidden + mixed, 0.0).astype(jnp.bfloat16)
        inverse = jnp.argsort(mapping).astype(jnp.int32)
        blocks = context_output.reshape(device_count, block_rows, 2 * key_span_width)[inverse]
        return (result, blocks)
    results, blocks = lax.map(one_request, (hidden_in.reshape(REQUEST_TOTAL, NEW_TOKEN_SLOTS, MODEL_WIDTH), prior_cache, cache_len, group_len, page_map))
    return (results.reshape(REQUEST_TOTAL * NEW_TOKEN_SLOTS, MODEL_WIDTH), jnp.transpose(blocks, (1, 0, 2, 3)))
```

```python
import functools

import jax
import jax.numpy as jnp
from jax import lax
from jax.experimental import pallas as pl
from jax.experimental.pallas import tpu as pltpu
from jax.sharding import PartitionSpec as P

QUERY_HEAD_COUNT = 20
KEY_VALUE_HEADS = 5
HEAD_SIZE = 64
GROUP = QUERY_HEAD_COUNT // KEY_VALUE_HEADS
NEW_TOKEN_SLOTS = 1024
PRIOR_SLOTS = 7168
SPAN = KEY_VALUE_HEADS * HEAD_SIZE
WIDTH = 2 * SPAN
LANES = 128
WINDOW = 256
LOCAL = 5
QUERY_ROWS = 256
QUERY_BLOCKS = NEW_TOKEN_SLOTS // QUERY_ROWS
STACK = LOCAL * QUERY_ROWS
KEY_ROWS = 1024
PROJECT_ROWS = 512
BLOCK_ROWS = 64
MIB = 1 << 20


def lane_ids(rows):
    return lax.broadcasted_iota(jnp.int32, (rows, LANES), 1)


def local_kv(rank, head):
    return (rank * LOCAL + head) // GROUP - rank


def key_tile_start(rank):
    return rank // 2


def value_tile_start(rank):
    return jnp.where(rank == 0, 2, 3)


def key_offset(rank):
    return rank * HEAD_SIZE - key_tile_start(rank) * LANES


def value_offset(rank):
    return SPAN + rank * HEAD_SIZE - value_tile_start(rank) * LANES


def rotate(tile, cosine, sine):
    low = lane_ids(tile.shape[0]) % HEAD_SIZE < HEAD_SIZE // 2
    half = HEAD_SIZE // 2
    other = jnp.where(low, pltpu.roll(tile, LANES - half, 1), pltpu.roll(tile, half, 1))
    return tile * cosine + other * sine


def project_kernel(
    scalars, hidden, gain, w_query, w_keyval, cosine, sine, queries, keyval, mixed_q, mixed_kv
):
    rank = scalars[2]
    fresh = scalars[1]

    @pl.when(pl.program_id(0) * PROJECT_ROWS < fresh)
    def _():
        value = hidden[...].astype(jnp.float32)
        scale = lax.rsqrt(jnp.mean(value * value, axis=-1, keepdims=True) + 1e-05)
        normed = (value * scale * gain[...].astype(jnp.float32)).astype(jnp.bfloat16)
        mixed_kv[...] = jnp.dot(normed, w_keyval[...], preferred_element_type=jnp.float32)
        mixed_q[:, :SPAN] = jnp.dot(normed, w_query[...], preferred_element_type=jnp.float32)
        cos, sin = cosine[...], sine[...]
        lanes = lane_ids(PROJECT_ROWS)
        for tile in range(WIDTH // LANES):
            columns = slice(tile * LANES, (tile + 1) * LANES)
            raw = mixed_kv[:, columns]
            if tile < 2:
                raw = rotate(raw, cos, sin)
            elif tile == 2:
                raw = jnp.where(lanes < HEAD_SIZE, rotate(raw, cos, sin), raw)
            keyval[:, columns] = raw.astype(jnp.bfloat16)
        turned = [
            rotate(mixed_q[:, tile * LANES : (tile + 1) * LANES], cos, sin) * HEAD_SIZE**-0.5
            for tile in range(3)
        ]
        swapped = [pltpu.roll(tile, HEAD_SIZE, 1) for tile in turned]
        for head in range(LOCAL):
            offset = key_offset(rank) + local_kv(rank, head) * HEAD_SIZE
            parity = (offset // HEAD_SIZE) % 2
            source = jnp.where(parity == head % 2, turned[head // 2], swapped[head // 2])
            source = jnp.where(lanes // HEAD_SIZE == parity, source, 0.0)
            for tile in range(2):
                placed = jnp.where(offset // LANES == tile, source, 0.0).astype(jnp.bfloat16)
                for part in range(PROJECT_ROWS // QUERY_ROWS):
                    queries[
                        part,
                        head * QUERY_ROWS : (head + 1) * QUERY_ROWS,
                        tile * LANES : (tile + 1) * LANES,
                    ] = placed[part * QUERY_ROWS : (part + 1) * QUERY_ROWS]

    @pl.when(pl.program_id(0) * PROJECT_ROWS >= fresh)
    def _():
        keyval[...] = jnp.zeros_like(keyval)
        queries[...] = jnp.zeros_like(queries)


def project(scalars, hidden_in, norm_gain, w_query, w_keyval, cosine, sine):
    rows, model = hidden_in.shape
    steps = rows // PROJECT_ROWS
    parts = PROJECT_ROWS // QUERY_ROWS
    return pl.pallas_call(
        project_kernel,
        out_shape=(
            jax.ShapeDtypeStruct((QUERY_BLOCKS, STACK, WINDOW), jnp.bfloat16),
            jax.ShapeDtypeStruct((rows, WIDTH), jnp.bfloat16),
        ),
        grid_spec=pltpu.PrefetchScalarGridSpec(
            num_scalar_prefetch=1,
            grid=(steps,),
            in_specs=[
                pl.BlockSpec((PROJECT_ROWS, model), lambda i, s: (i, 0)),
                pl.BlockSpec((1, model), lambda i, s: (0, 0)),
                pl.BlockSpec(w_query.shape, lambda i, s: (0, 0)),
                pl.BlockSpec(w_keyval.shape, lambda i, s: (0, 0)),
                pl.BlockSpec((PROJECT_ROWS, LANES), lambda i, s: (i, 0)),
                pl.BlockSpec((PROJECT_ROWS, LANES), lambda i, s: (i, 0)),
            ],
            out_specs=[
                pl.BlockSpec((parts, STACK, WINDOW), lambda i, s: (i, 0, 0)),
                pl.BlockSpec((PROJECT_ROWS, WIDTH), lambda i, s: (i, 0)),
            ],
            scratch_shapes=[
                pltpu.VMEM((PROJECT_ROWS, 3 * LANES), jnp.float32),
                pltpu.VMEM((PROJECT_ROWS, WIDTH), jnp.float32),
            ],
        ),
        compiler_params=pltpu.CompilerParams(vmem_limit_bytes=48 * MIB),
        cost_estimate=pl.CostEstimate(
            flops=2 * rows * model * 960, bytes_accessed=12 * MIB, transcendentals=0
        ),
        name="project",
    )(scalars, hidden_in, norm_gain.reshape(1, -1), w_query, w_keyval, cosine, sine)


def pick_kernel(scalars, picks, prior, keyval, outgoing, semaphores):
    cached, fresh = scalars[0], scalars[1]
    count = outgoing.shape[0]
    prior_blocks = PRIOR_SLOTS // BLOCK_ROWS

    def live_rows(block):
        return jnp.where(
            block < prior_blocks,
            cached - block * BLOCK_ROWS,
            fresh - (block - prior_blocks) * BLOCK_ROWS,
        )

    for slot in range(count):
        block = picks[slot]

        @pl.when((block < prior_blocks) & (live_rows(block) > 0))
        def _():
            start = pl.multiple_of(block * BLOCK_ROWS, BLOCK_ROWS)
            pltpu.make_async_copy(
                prior.at[pl.ds(start, BLOCK_ROWS)], outgoing.at[slot], semaphores.at[slot]
            ).start()

        @pl.when((block >= prior_blocks) & (live_rows(block) > 0))
        def _():
            start = pl.multiple_of((block - prior_blocks) * BLOCK_ROWS, BLOCK_ROWS)
            pltpu.make_async_copy(
                keyval.at[pl.ds(start, BLOCK_ROWS)], outgoing.at[slot], semaphores.at[slot]
            ).start()

    for slot in range(count):
        live = live_rows(picks[slot])

        @pl.when(live <= 0)
        def _():
            outgoing[slot] = jnp.zeros((BLOCK_ROWS, WIDTH), jnp.bfloat16)

        @pl.when(live > 0)
        def _():
            pltpu.make_async_copy(
                prior.at[pl.ds(0, BLOCK_ROWS)], outgoing.at[slot], semaphores.at[slot]
            ).wait()

        @pl.when((live > 0) & (live < BLOCK_ROWS))
        def _():
            rows = lax.broadcasted_iota(jnp.int32, (BLOCK_ROWS, WIDTH), 0)
            value = outgoing[slot].astype(jnp.float32)
            outgoing[slot] = jnp.where(rows < live, value, 0.0).astype(jnp.bfloat16)


def pick_blocks(scalars, picks, prior, keyval):
    count = picks.shape[0]
    return pl.pallas_call(
        pick_kernel,
        out_shape=jax.ShapeDtypeStruct((count, BLOCK_ROWS, WIDTH), jnp.bfloat16),
        grid_spec=pltpu.PrefetchScalarGridSpec(
            num_scalar_prefetch=2,
            grid=(1,),
            in_specs=[pl.BlockSpec(memory_space=pl.ANY), pl.BlockSpec(memory_space=pl.ANY)],
            out_specs=pl.BlockSpec((count, BLOCK_ROWS, WIDTH), lambda i, s, p: (0, 0, 0)),
            scratch_shapes=[pltpu.SemaphoreType.DMA((count,))],
        ),
        compiler_params=pltpu.CompilerParams(vmem_limit_bytes=16 * MIB),
        cost_estimate=pl.CostEstimate(flops=0, bytes_accessed=5 * MIB, transcendentals=0),
        name="pick_blocks",
    )(scalars, picks, prior, keyval)


def attend_kernel(
    scalars, queries, prior, fresh_rows, heads_out, keys, values, top, total, semaphores
):
    cached, fresh, rank = scalars[0], scalars[1], scalars[2]
    key_start = pl.multiple_of(key_tile_start(rank) * LANES, LANES)
    value_start = pl.multiple_of(value_tile_start(rank) * LANES, LANES)
    first = value_offset(rank)
    prior_chunks = (cached + KEY_ROWS - 1) // KEY_ROWS
    blocks = (fresh + QUERY_ROWS - 1) // QUERY_ROWS
    chunk_limit = PRIOR_SLOTS // KEY_ROWS

    def copies(chunk):
        into = pl.ds(chunk * KEY_ROWS, KEY_ROWS)
        if isinstance(chunk, int) and chunk == chunk_limit:
            source, rows = fresh_rows, pl.ds(0, NEW_TOKEN_SLOTS)
        else:
            source, rows = prior, into
        return (
            pltpu.make_async_copy(
                source.at[rows, pl.ds(key_start, WINDOW)], keys.at[into], semaphores.at[0, chunk]
            ),
            pltpu.make_async_copy(
                source.at[rows, pl.ds(value_start, WINDOW)],
                values.at[into],
                semaphores.at[1, chunk],
            ),
        )

    for copy in copies(chunk_limit):
        copy.start()
    for chunk in range(chunk_limit):

        @pl.when(chunk < prior_chunks)
        def _():
            for copy in copies(chunk):
                copy.start()

    def widen(start, rows):
        lanes = lax.broadcasted_iota(jnp.int32, (rows, WINDOW), 1)
        here = pl.ds(start, rows)
        own = (lanes >= first) & (lanes < first + 2 * HEAD_SIZE)
        raw = values[here].astype(jnp.float32)
        values[here] = jnp.where(own, raw, 1.0).astype(jnp.bfloat16)

    def arrive(chunk):
        start = pl.multiple_of(chunk * KEY_ROWS, KEY_ROWS)
        for copy in copies(chunk):
            copy.wait()
        widen(start, KEY_ROWS)
        live = cached - start

        @pl.when(live < KEY_ROWS)
        def _():
            here = pl.ds(start, KEY_ROWS)
            rows = lax.broadcasted_iota(jnp.int32, (KEY_ROWS, WINDOW), 0)
            spare = keys[0:8].astype(jnp.float32)[0:1]
            raw = keys[here].astype(jnp.float32)
            keys[here] = jnp.where(rows < live, raw, spare).astype(jnp.bfloat16)
            raw = values[here].astype(jnp.float32)
            values[here] = jnp.where(rows < live, raw, 0.0).astype(jnp.bfloat16)

    def absorb(block, start, rows, masked):
        here = pl.ds(start, rows)
        for head in range(LOCAL):
            own = slice(head * QUERY_ROWS, (head + 1) * QUERY_ROWS)
            scores = lax.dot_general(
                queries[block, own, :],
                keys[here],
                (((1,), (1,)), ((), ())),
                preferred_element_type=jnp.float32,
            )
            if masked:
                row = lax.broadcasted_iota(jnp.int32, scores.shape, 0)
                column = lax.broadcasted_iota(jnp.int32, scores.shape, 1)
                scores = jnp.where(column <= row, scores, -1e30)
            before = top[own]
            after = jnp.maximum(before, jnp.max(scores, axis=-1, keepdims=True))
            rescale = jnp.exp(before - after)
            chances = jnp.exp(scores - jnp.tile(after, (1, rows // LANES)))
            chances = chances.astype(jnp.bfloat16)
            top[own] = after
            total[own] = total[own] * jnp.tile(rescale, (1, WINDOW // LANES)) + jnp.dot(
                chances, values[here], preferred_element_type=jnp.float32
            )

    def query_block(block, carry):
        top[...] = jnp.full_like(top, -1e30)
        total[...] = jnp.zeros_like(total)

        @pl.when(block == 0)
        def _():
            for copy in copies(chunk_limit):
                copy.wait()
            widen(PRIOR_SLOTS, NEW_TOKEN_SLOTS)

        def earlier(step, inner):
            start = pl.multiple_of(PRIOR_SLOTS + step * QUERY_ROWS, QUERY_ROWS)
            absorb(block, start, QUERY_ROWS, False)
            return inner

        def cache(step, inner):
            @pl.when(block == 0)
            def _():
                arrive(step)

            start = pl.multiple_of(step * KEY_ROWS, KEY_ROWS)
            absorb(block, start, KEY_ROWS, False)
            return inner

        start = pl.multiple_of(PRIOR_SLOTS + block * QUERY_ROWS, QUERY_ROWS)
        absorb(block, start, QUERY_ROWS, True)
        lax.fori_loop(0, block, earlier, 0)
        lax.fori_loop(0, prior_chunks, cache, 0)

        lanes = lane_ids(QUERY_ROWS)
        spare = jnp.where(first == 0, LANES, 0)
        spare_tile = spare // LANES
        picked = []
        for head in range(LOCAL):
            own = slice(head * QUERY_ROWS, (head + 1) * QUERY_ROWS)
            low, high = total[own, :LANES], total[own, LANES:]
            counts = jnp.where(spare_tile == 0, low, high)
            denom = jnp.sum(jnp.where(lanes == 0, counts, 0.0), axis=-1, keepdims=True)
            offset = first + local_kv(rank, head) * HEAD_SIZE
            parity = (offset // HEAD_SIZE) % 2
            chosen = jnp.where(offset // LANES == 0, low, high)
            chosen = jnp.where(parity == head % 2, chosen, pltpu.roll(chosen, HEAD_SIZE, 1))
            picked.append(chosen / denom)
        here = pl.ds(pl.multiple_of(block * QUERY_ROWS, QUERY_ROWS), QUERY_ROWS)
        for tile in range(2):
            pair = jnp.where(lanes < HEAD_SIZE, picked[2 * tile], picked[2 * tile + 1])
            heads_out[here, tile * LANES : (tile + 1) * LANES] = pair.astype(jnp.bfloat16)
        heads_out[here, 2 * LANES :] = picked[4][:, :HEAD_SIZE].astype(jnp.bfloat16)
        return carry

    lax.fori_loop(0, blocks, query_block, 0)

    def idle(block, carry):
        here = pl.ds(pl.multiple_of(block * QUERY_ROWS, QUERY_ROWS), QUERY_ROWS)
        heads_out[here] = jnp.zeros((QUERY_ROWS, LOCAL * HEAD_SIZE), jnp.bfloat16)
        return carry

    lax.fori_loop(blocks, QUERY_BLOCKS, idle, 0)


def attend(scalars, queries, prior, fresh_rows):
    chunks = PRIOR_SLOTS // KEY_ROWS + 1
    return pl.pallas_call(
        attend_kernel,
        out_shape=jax.ShapeDtypeStruct((NEW_TOKEN_SLOTS, LOCAL * HEAD_SIZE), jnp.bfloat16),
        grid_spec=pltpu.PrefetchScalarGridSpec(
            num_scalar_prefetch=1,
            grid=(1,),
            in_specs=[
                pl.BlockSpec(queries.shape, lambda i, s: (0, 0, 0)),
                pl.BlockSpec(memory_space=pl.ANY),
                pl.BlockSpec(memory_space=pl.ANY),
            ],
            out_specs=pl.BlockSpec((NEW_TOKEN_SLOTS, LOCAL * HEAD_SIZE), lambda i, s: (0, 0)),
            scratch_shapes=[
                pltpu.VMEM((PRIOR_SLOTS + NEW_TOKEN_SLOTS, WINDOW), jnp.bfloat16),
                pltpu.VMEM((PRIOR_SLOTS + NEW_TOKEN_SLOTS, WINDOW), jnp.bfloat16),
                pltpu.VMEM((STACK, LANES), jnp.float32),
                pltpu.VMEM((STACK, WINDOW), jnp.float32),
                pltpu.SemaphoreType.DMA((2, chunks)),
            ],
        ),
        compiler_params=pltpu.CompilerParams(vmem_limit_bytes=48 * MIB),
        cost_estimate=pl.CostEstimate(
            flops=4 * 5120 * 7680 * 256, bytes_accessed=12 * MIB, transcendentals=5120 * 7680
        ),
        name="attend",
    )(scalars, queries, prior, fresh_rows)


def finish_kernel(scalars, heads, w_out, hidden, result):
    rank, fresh = scalars[2], scalars[1]
    mixed = jnp.zeros(result.shape, jnp.float32)
    for part in range(heads.shape[0]):
        mixed = mixed + jnp.dot(
            heads[part], w_out[part], preferred_element_type=jnp.float32
        )
    rows = lax.broadcasted_iota(jnp.int32, result.shape, 0) + rank * result.shape[0]
    value = hidden[...].astype(jnp.float32) + mixed
    result[...] = jnp.where(rows < fresh, value, 0.0).astype(jnp.bfloat16)


def finish(scalars, heads, w_out, hidden_in):
    parts, rows, columns = heads.shape
    model = w_out.shape[1]
    tile = 512
    return pl.pallas_call(
        finish_kernel,
        out_shape=jax.ShapeDtypeStruct((rows, model), jnp.bfloat16),
        grid_spec=pltpu.PrefetchScalarGridSpec(
            num_scalar_prefetch=1,
            grid=(model // tile,),
            in_specs=[
                pl.BlockSpec(heads.shape, lambda i, s: (0, 0, 0)),
                pl.BlockSpec((parts, columns, tile), lambda i, s: (0, 0, i)),
                pl.BlockSpec((rows, tile), lambda i, s: (s[2], i)),
            ],
            out_specs=pl.BlockSpec((rows, tile), lambda i, s: (0, i)),
        ),
        compiler_params=pltpu.CompilerParams(vmem_limit_bytes=32 * MIB),
        cost_estimate=pl.CostEstimate(
            flops=2 * rows * parts * columns * model, bytes_accessed=8 * MIB, transcendentals=0
        ),
        name="finish",
    )(scalars, heads, w_out.reshape(parts, columns, model), hidden_in)


def shards(
    hidden_in,
    norm_gain,
    w_query,
    key_value_weight,
    w_out,
    prior_cache,
    cache_len,
    group_len,
    page_map,
):
    rank = lax.axis_index("tp").astype(jnp.int32)
    tp_count = lax.axis_size("tp")
    req_count = lax.axis_size("req")
    scalars = jnp.stack([cache_len[0], group_len[0], rank])

    half_size = HEAD_SIZE // 2
    frequency = 10000.0 ** (-(jnp.arange(half_size, dtype=jnp.float32) * 2.0 / HEAD_SIZE))
    positions = cache_len[0] + jnp.arange(NEW_TOKEN_SLOTS, dtype=jnp.int32)
    angles = positions.astype(jnp.float32)[:, None] * jnp.tile(frequency, 4)[None, :]
    sign = jnp.where(jnp.arange(LANES) % HEAD_SIZE < half_size, -1.0, 1.0)
    cosine = jnp.cos(angles)
    sine = jnp.sin(angles) * sign[None, :]

    targets = jnp.arange(req_count, dtype=jnp.int32) * tp_count + rank
    order = jnp.arange(page_map.shape[1], dtype=jnp.int32)
    picks = jnp.sum(
        jnp.where(page_map[0][None, :] == targets[:, None], order[None, :], 0), axis=1
    ).astype(jnp.int32)

    prior = prior_cache[0]
    queries, keyval = project(
        scalars, hidden_in, norm_gain, w_query, key_value_weight, cosine, sine
    )
    outgoing = pick_blocks(scalars, picks, prior, keyval)
    received = lax.all_to_all(outgoing, "req", split_axis=0, concat_axis=0, tiled=True)
    decode_kv = received[None]
    attended = attend(scalars, queries, prior, keyval)
    parts = attended.reshape(tp_count, NEW_TOKEN_SLOTS // tp_count, LOCAL * HEAD_SIZE)
    heads = lax.all_to_all(parts, "tp", split_axis=0, concat_axis=0, tiled=True)
    hidden_out = finish(scalars, heads, w_out, hidden_in)
    return (hidden_out, decode_kv)


def solution(mesh):
    placed = (
        P("req", None),
        P(),
        P(None, "tp"),
        P(),
        P(),
        P("req", None, None),
        P("req"),
        P("req"),
        P("req", None),
    )
    return jax.shard_map(
        shards,
        mesh=mesh,
        in_specs=placed,
        out_specs=(P(("req", "tp"), None), P(("req", "tp"), None, None, None)),
        check_vma=False,
    )
```

```python
import jax
import jax.numpy as jnp
from jax import lax
from jax.experimental import pallas as pl
from jax.experimental.pallas import tpu as pltpu
from jax.sharding import PartitionSpec as P

QUERY_HEAD_COUNT = 20
KEY_VALUE_HEADS = 5
HEAD_SIZE = 64
GROUP = QUERY_HEAD_COUNT // KEY_VALUE_HEADS
NEW_TOKEN_SLOTS = 1024
PRIOR_SLOTS = 7168
SPAN = KEY_VALUE_HEADS * HEAD_SIZE
WIDTH = 2 * SPAN
LANES = 128
WINDOW = 256
LOCAL = 5
QUERY_ROWS = 512
QUERY_BLOCKS = NEW_TOKEN_SLOTS // QUERY_ROWS
STACK = LOCAL * QUERY_ROWS
KEY_ROWS = 1024
PREPARE_ROWS = 256
PROJECT_ROWS = 512
NORM_ROWS = 256
PART_ROWS = 256
FINISH_COLUMNS = 512
PACKED = PART_ROWS * LOCAL // 2
BLOCK_ROWS = 64
MIB = 1 << 20


def lane_ids(rows):
    return lax.broadcasted_iota(jnp.int32, (rows, LANES), 1)


def local_kv(rank, head):
    return (rank * LOCAL + head) // GROUP - rank


def key_tile_start(rank):
    return rank // 2


def value_tile_start(rank):
    return jnp.where(rank == 0, 2, 3)


def key_offset(rank):
    return rank * HEAD_SIZE - key_tile_start(rank) * LANES


def value_offset(rank):
    return SPAN + rank * HEAD_SIZE - value_tile_start(rank) * LANES


def rotate(tile, cosine, sine):
    low = lane_ids(tile.shape[0]) % HEAD_SIZE < HEAD_SIZE // 2
    half = HEAD_SIZE // 2
    other = jnp.where(low, pltpu.roll(tile, LANES - half, 1), pltpu.roll(tile, half, 1))
    return tile * cosine + other * sine


def project_kernel(
    hidden_hbm,
    gain,
    w_query_hbm,
    w_keyval_hbm,
    cosine,
    sine,
    queries,
    keyval,
    hidden,
    w_query,
    w_keyval,
    normed,
    mixed_q,
    mixed_kv,
    semaphores,
):
    total = hidden.shape[0]
    pieces = total // NORM_ROWS
    loads = [
        pltpu.make_async_copy(
            hidden_hbm.at[pl.ds(piece * NORM_ROWS, NORM_ROWS)],
            hidden.at[pl.ds(piece * NORM_ROWS, NORM_ROWS)],
            semaphores.at[piece],
        )
        for piece in range(pieces)
    ]
    weights = [
        pltpu.make_async_copy(w_keyval_hbm, w_keyval, semaphores.at[pieces]),
        pltpu.make_async_copy(w_query_hbm, w_query, semaphores.at[pieces + 1]),
    ]
    for copy in loads[:2] + weights + loads[2:]:
        copy.start()

    def norm(piece):
        here = pl.ds(piece * NORM_ROWS, NORM_ROWS)
        value = hidden[here].astype(jnp.float32)
        scale = lax.rsqrt(jnp.mean(value * value, axis=-1, keepdims=True) + 1e-05)
        normed[here] = (value * scale * gain[...].astype(jnp.float32)).astype(jnp.bfloat16)

    lanes = lane_ids(PROJECT_ROWS)

    def mix(block):
        here = pl.ds(block * PROJECT_ROWS, PROJECT_ROWS)
        rows = normed[here]
        mixed_kv[here] = jnp.dot(rows, w_keyval[...], preferred_element_type=jnp.float32)
        mixed_q[here, :SPAN] = lax.dot_general(
            rows, w_query[...], (((1,), (1,)), ((), ())), preferred_element_type=jnp.float32
        )

    def turn(block):
        here = pl.ds(block * PROJECT_ROWS, PROJECT_ROWS)
        cos, sin = cosine[here], sine[here]
        for tile in range(WIDTH // LANES):
            columns = slice(tile * LANES, (tile + 1) * LANES)
            raw = mixed_kv[here, columns]
            if tile < 2:
                raw = rotate(raw, cos, sin)
            elif tile == 2:
                raw = jnp.where(lanes < HEAD_SIZE, rotate(raw, cos, sin), raw)
            keyval[here, columns] = raw.astype(jnp.bfloat16)
        for head in range(LOCAL):
            tile = head // 2
            raw = mixed_q[here, tile * LANES : (tile + 1) * LANES]
            turned = rotate(raw, cos, sin) * HEAD_SIZE**-0.5
            if head % 2:
                turned = pltpu.roll(turned, HEAD_SIZE, 1)
            queries[block, head * QUERY_ROWS : (head + 1) * QUERY_ROWS] = turned[
                :, :HEAD_SIZE
            ].astype(jnp.bfloat16)

    for piece in range(2):
        loads[piece].wait()
        norm(piece)
    for copy in weights + loads[2:]:
        copy.wait()
    mix(0)
    norm(2)
    norm(3)
    mix(1)
    turn(0)
    turn(1)


def project(hidden_in, norm_gain, w_query, w_keyval, cosine, sine):
    rows, model = hidden_in.shape
    vector = pl.BlockSpec(memory_space=pltpu.VMEM)
    far = pl.BlockSpec(memory_space=pltpu.HBM)
    return pl.pallas_call(
        project_kernel,
        out_shape=(
            jax.ShapeDtypeStruct((QUERY_BLOCKS, STACK, HEAD_SIZE), jnp.bfloat16),
            jax.ShapeDtypeStruct((rows, WIDTH), jnp.bfloat16),
        ),
        in_specs=[far, vector, far, far, vector, vector],
        out_specs=[vector, vector],
        scratch_shapes=[
            pltpu.VMEM((rows, model), jnp.bfloat16),
            pltpu.VMEM((SPAN, model), jnp.bfloat16),
            pltpu.VMEM((model, WIDTH), jnp.bfloat16),
            pltpu.VMEM((rows, model), jnp.bfloat16),
            pltpu.VMEM((rows, 3 * LANES), jnp.float32),
            pltpu.VMEM((rows, WIDTH), jnp.float32),
            pltpu.SemaphoreType.DMA((rows // NORM_ROWS + 2,)),
        ],
        compiler_params=pltpu.CompilerParams(vmem_limit_bytes=58 * MIB),
        cost_estimate=pl.CostEstimate(
            flops=2 * rows * model * (SPAN + WIDTH), bytes_accessed=10 * MIB, transcendentals=0
        ),
        name="project",
    )(hidden_in, norm_gain.reshape(1, -1), w_query.T, w_keyval, cosine, sine)


def pick_kernel(scalars, picks, prior, keyval, outgoing, semaphores):
    cached, fresh = scalars[0], scalars[1]
    count = outgoing.shape[0]
    prior_blocks = PRIOR_SLOTS // BLOCK_ROWS

    def live_rows(block):
        return jnp.where(
            block < prior_blocks,
            cached - block * BLOCK_ROWS,
            fresh - (block - prior_blocks) * BLOCK_ROWS,
        )

    for slot in range(count):
        block = picks[slot]

        @pl.when((block < prior_blocks) & (live_rows(block) > 0))
        def _():
            start = pl.multiple_of(block * BLOCK_ROWS, BLOCK_ROWS)
            pltpu.make_async_copy(
                prior.at[pl.ds(start, BLOCK_ROWS)], outgoing.at[slot], semaphores.at[slot]
            ).start()

        @pl.when((block >= prior_blocks) & (live_rows(block) > 0))
        def _():
            start = pl.multiple_of((block - prior_blocks) * BLOCK_ROWS, BLOCK_ROWS)
            pltpu.make_async_copy(
                keyval.at[pl.ds(start, BLOCK_ROWS)], outgoing.at[slot], semaphores.at[slot]
            ).start()

    for slot in range(count):
        live = live_rows(picks[slot])

        @pl.when(live <= 0)
        def _():
            outgoing[slot] = jnp.zeros((BLOCK_ROWS, WIDTH), jnp.bfloat16)

        @pl.when(live > 0)
        def _():
            pltpu.make_async_copy(
                prior.at[pl.ds(0, BLOCK_ROWS)], outgoing.at[slot], semaphores.at[slot]
            ).wait()

        @pl.when((live > 0) & (live < BLOCK_ROWS))
        def _():
            rows = lax.broadcasted_iota(jnp.int32, (BLOCK_ROWS, WIDTH), 0)
            value = outgoing[slot].astype(jnp.float32)
            outgoing[slot] = jnp.where(rows < live, value, 0.0).astype(jnp.bfloat16)


def pick_blocks(scalars, picks, prior, keyval):
    count = picks.shape[0]
    return pl.pallas_call(
        pick_kernel,
        out_shape=jax.ShapeDtypeStruct((count, BLOCK_ROWS, WIDTH), jnp.bfloat16),
        grid_spec=pltpu.PrefetchScalarGridSpec(
            num_scalar_prefetch=2,
            grid=(1,),
            in_specs=[
                pl.BlockSpec(memory_space=pltpu.HBM),
                pl.BlockSpec(memory_space=pl.ANY),
            ],
            out_specs=pl.BlockSpec((count, BLOCK_ROWS, WIDTH), lambda i, s, p: (0, 0, 0)),
            scratch_shapes=[pltpu.SemaphoreType.DMA((count,))],
        ),
        compiler_params=pltpu.CompilerParams(vmem_limit_bytes=56 * MIB),
        cost_estimate=pl.CostEstimate(flops=0, bytes_accessed=5 * MIB, transcendentals=0),
        name="pick_blocks",
    )(scalars, picks, prior, keyval)


def attend_kernel(
    scalars,
    queries,
    prior,
    fresh_rows,
    heads_out,
    raw_keys,
    raw_values,
    keys,
    values,
    top,
    total,
    semaphores,
):
    cached, fresh, rank = scalars[0], scalars[1], scalars[2]
    key_start = pl.multiple_of(key_tile_start(rank) * LANES, LANES)
    value_start = pl.multiple_of(value_tile_start(rank) * LANES, LANES)
    key_shift, value_shift = key_offset(rank), value_offset(rank)
    prior_chunks = (cached + KEY_ROWS - 1) // KEY_ROWS
    blocks = (fresh + QUERY_ROWS - 1) // QUERY_ROWS
    chunk_limit = PRIOR_SLOTS // KEY_ROWS

    def copies(chunk):
        into = pl.ds(chunk * KEY_ROWS, KEY_ROWS)
        return (
            pltpu.make_async_copy(
                prior.at[into, pl.ds(key_start, WINDOW)],
                raw_keys.at[into],
                semaphores.at[0, chunk],
            ),
            pltpu.make_async_copy(
                prior.at[into, pl.ds(value_start, WINDOW)],
                raw_values.at[into],
                semaphores.at[1, chunk],
            ),
        )

    into = pl.ds(PRIOR_SLOTS, NEW_TOKEN_SLOTS)
    fresh_copies = (
        pltpu.make_async_copy(
            fresh_rows.at[:, pl.ds(key_start, WINDOW)],
            raw_keys.at[into],
            semaphores.at[0, chunk_limit],
        ),
        pltpu.make_async_copy(
            fresh_rows.at[:, pl.ds(value_start, WINDOW)],
            raw_values.at[into],
            semaphores.at[1, chunk_limit],
        ),
    )
    for copy in fresh_copies:
        copy.start()
    for chunk in range(chunk_limit):

        @pl.when(chunk < prior_chunks)
        def _():
            for copy in copies(chunk):
                copy.start()

    def prepare(start, live):
        here = pl.ds(start, PREPARE_ROWS)
        lanes = lane_ids(PREPARE_ROWS)
        alive = lax.broadcasted_iota(jnp.int32, (PREPARE_ROWS, LANES), 0) < live
        raw = raw_keys[here].astype(jnp.float32)
        low, high = raw[:, :LANES], raw[:, LANES:]
        spare = raw_keys[0:8].astype(jnp.float32)[0:1]
        low = jnp.where(alive, low, spare[:, :LANES])
        high = jnp.where(alive, high, spare[:, LANES:])
        joined = jnp.where(
            lanes < HEAD_SIZE, pltpu.roll(low, HEAD_SIZE, 1), pltpu.roll(high, HEAD_SIZE, 1)
        )
        pair = jnp.where(key_shift == 0, low, joined)
        keys[:, here] = pair.T.astype(jnp.bfloat16)
        raw = raw_values[here].astype(jnp.float32)
        low, high = raw[:, :LANES], raw[:, LANES:]
        low_turned, high_turned = pltpu.roll(low, HEAD_SIZE, 1), pltpu.roll(high, HEAD_SIZE, 1)
        one = jnp.where(
            value_shift == 0, low, jnp.where(value_shift == HEAD_SIZE, low_turned, high)
        )
        two = jnp.where(
            value_shift == 0, low_turned, jnp.where(value_shift == HEAD_SIZE, high, high_turned)
        )
        for slot, own in enumerate((one, two)):
            own = jnp.where(alive, jnp.where(lanes < HEAD_SIZE, own, 1.0), 0.0)
            values[slot, here] = own.astype(jnp.bfloat16)

    def score(block, head, start, rows):
        which = local_kv(rank, head)
        return jnp.dot(
            queries[block, head * QUERY_ROWS : (head + 1) * QUERY_ROWS],
            keys[pl.ds(pl.multiple_of(which * HEAD_SIZE, HEAD_SIZE), HEAD_SIZE), pl.ds(start, rows)],
            preferred_element_type=jnp.float32,
        )

    def blend(head, start, rows, scores, masked):
        own = slice(head * QUERY_ROWS, (head + 1) * QUERY_ROWS)
        if masked:
            row = lax.broadcasted_iota(jnp.int32, scores.shape, 0)
            column = lax.broadcasted_iota(jnp.int32, scores.shape, 1)
            scores = jnp.where(column <= row, scores, -1e30)
        before = top[own]
        after = jnp.maximum(before, jnp.max(scores, axis=-1, keepdims=True))
        rescale = jnp.exp(before - after)
        chances = jnp.exp(scores - jnp.tile(after, (1, rows // LANES))).astype(jnp.bfloat16)
        top[own] = after
        total[own] = total[own] * rescale + jnp.dot(
            chances,
            values[local_kv(rank, head), pl.ds(start, rows)],
            preferred_element_type=jnp.float32,
        )

    def absorb(block, start, rows, masked):
        pending = score(block, 0, start, rows)
        for head in range(LOCAL):
            following = score(block, head + 1, start, rows) if head + 1 < LOCAL else None
            blend(head, start, rows, pending, masked)
            pending = following

    def query_block(block, carry):
        top[...] = jnp.full_like(top, -1e30)
        total[...] = jnp.zeros_like(total)

        @pl.when(block == 0)
        def _():
            for copy in fresh_copies:
                copy.wait()

            def each(step, inner):
                start = pl.multiple_of(PRIOR_SLOTS + step * PREPARE_ROWS, PREPARE_ROWS)
                prepare(start, PREPARE_ROWS)
                return inner

            lax.fori_loop(0, NEW_TOKEN_SLOTS // PREPARE_ROWS, each, 0)

        def earlier(step, inner):
            start = pl.multiple_of(PRIOR_SLOTS + step * QUERY_ROWS, QUERY_ROWS)
            absorb(block, start, QUERY_ROWS, False)
            return inner

        def cache(step, inner):
            start = pl.multiple_of(step * KEY_ROWS, KEY_ROWS)

            @pl.when(block == 0)
            def _():
                for copy in copies(step):
                    copy.wait()

                def each(part, most):
                    here = pl.multiple_of(start + part * PREPARE_ROWS, PREPARE_ROWS)
                    prepare(here, cached - here)
                    return most

                lax.fori_loop(0, KEY_ROWS // PREPARE_ROWS, each, 0)

            absorb(block, start, KEY_ROWS, False)
            return inner

        start = pl.multiple_of(PRIOR_SLOTS + block * QUERY_ROWS, QUERY_ROWS)
        absorb(block, start, QUERY_ROWS, True)
        lax.fori_loop(0, block, earlier, 0)
        lax.fori_loop(0, prior_chunks, cache, 0)

        lanes = lane_ids(QUERY_ROWS)
        odd = rank % 2 == 1
        plain, turned = [], []
        for head in range(LOCAL):
            sums = total[head * QUERY_ROWS : (head + 1) * QUERY_ROWS]
            swapped = pltpu.roll(sums, HEAD_SIZE, 1)
            plain.append(sums / swapped)
            turned.append(swapped / sums)
        even_pairs = [jnp.where(lanes < HEAD_SIZE, plain[i], turned[i + 1]) for i in (0, 2)]
        odd_pairs = [jnp.where(lanes < HEAD_SIZE, plain[i], turned[i + 1]) for i in (1, 3)]
        single = jnp.where(odd, plain[0], plain[4])
        single_turned = jnp.where(odd, turned[0], turned[4])
        near = (lane_ids(LANES) < HEAD_SIZE) != odd
        for part in range(QUERY_ROWS // PART_ROWS):
            slot = block * (QUERY_ROWS // PART_ROWS) + part
            rows = slice(part * PART_ROWS, (part + 1) * PART_ROWS)
            for tile in range(2):
                pair = jnp.where(odd, odd_pairs[tile][rows], even_pairs[tile][rows])
                heads_out[slot, tile * PART_ROWS : (tile + 1) * PART_ROWS] = pair.astype(
                    jnp.bfloat16
                )
            begin = part * PART_ROWS
            above, below = slice(begin, begin + LANES), slice(begin + LANES, begin + PART_ROWS)
            packed = jnp.where(
                odd,
                jnp.where(near, single_turned[above], single[below]),
                jnp.where(near, single[above], single_turned[below]),
            )
            heads_out[slot, 2 * PART_ROWS :] = packed.astype(jnp.bfloat16)
        return carry

    lax.fori_loop(0, blocks, query_block, 0)

    def idle(slot, carry):
        heads_out[slot] = jnp.zeros((PACKED, LANES), jnp.bfloat16)
        return carry

    parts = QUERY_ROWS // PART_ROWS
    lax.fori_loop(blocks * parts, QUERY_BLOCKS * parts, idle, 0)


def attend(scalars, queries, prior, fresh_rows):
    context = PRIOR_SLOTS + NEW_TOKEN_SLOTS
    vector = pl.BlockSpec(memory_space=pltpu.VMEM)
    return pl.pallas_call(
        attend_kernel,
        out_shape=jax.ShapeDtypeStruct(
            (NEW_TOKEN_SLOTS // PART_ROWS, PACKED, LANES), jnp.bfloat16
        ),
        in_specs=[
            pl.BlockSpec(memory_space=pltpu.SMEM),
            vector,
            pl.BlockSpec(memory_space=pltpu.HBM),
            pl.BlockSpec(memory_space=pl.ANY),
        ],
        out_specs=vector,
        scratch_shapes=[
            pltpu.VMEM((context, WINDOW), jnp.bfloat16),
            pltpu.VMEM((context, WINDOW), jnp.bfloat16),
            pltpu.VMEM((LANES, context), jnp.bfloat16),
            pltpu.VMEM((2, context, LANES), jnp.bfloat16),
            pltpu.VMEM((STACK, LANES), jnp.float32),
            pltpu.VMEM((STACK, LANES), jnp.float32),
            pltpu.SemaphoreType.DMA((2, PRIOR_SLOTS // KEY_ROWS + 1)),
        ],
        compiler_params=pltpu.CompilerParams(vmem_limit_bytes=56 * MIB),
        cost_estimate=pl.CostEstimate(
            flops=4 * 5120 * 7680 * 256, bytes_accessed=12 * MIB, transcendentals=5120 * 7680
        ),
        name="attend",
    )(scalars, queries, prior, fresh_rows)


def finish_kernel(
    scalars,
    heads,
    w_out_hbm,
    hidden_hbm,
    received,
    result,
    decode,
    w_out,
    hidden,
    joined,
    semaphores,
    move_semaphores,
):
    rank, fresh = scalars[2], scalars[1]
    rows = result.shape[0]
    wide = FINISH_COLUMNS
    steps = result.shape[1] // wide
    loads = [
        pltpu.make_async_copy(
            w_out_hbm.at[:, pl.ds(step * wide, wide)], w_out.at[step], semaphores.at[step]
        )
        for step in range(steps)
    ]
    own_rows = pltpu.make_async_copy(
        hidden_hbm.at[pl.ds(pl.multiple_of(rank * rows, rows), rows)], hidden, semaphores.at[steps]
    )
    for copy in loads[:1] + [own_rows] + loads[1:]:
        copy.start()
    moves = [
        pltpu.make_async_copy(
            received.at[pl.ds(part * 8, 8)], decode.at[pl.ds(part * 8, 8)], move_semaphores.at[part]
        )
        for part in range(received.shape[0] // 8)
    ]
    for move in moves:
        move.start()
    low = lane_ids(LANES) < HEAD_SIZE
    for pair in range(2):
        first, second = heads.at[2 * pair], heads.at[2 * pair + 1]
        for tile in range(2):
            source = slice(tile * PART_ROWS, (tile + 1) * PART_ROWS)
            columns = (5 * pair + tile) * LANES
            joined[:, columns : columns + LANES] = first[source]
            joined[:, columns + 3 * LANES : columns + 4 * LANES] = second[source]
        one = first[2 * PART_ROWS :].astype(jnp.float32)
        two = second[2 * PART_ROWS :].astype(jnp.float32)
        columns = (5 * pair + 2) * LANES
        joined[:LANES, columns : columns + LANES] = jnp.where(low, one, two).astype(jnp.bfloat16)
        one, two = pltpu.roll(one, HEAD_SIZE, 1), pltpu.roll(two, HEAD_SIZE, 1)
        joined[LANES:, columns : columns + LANES] = jnp.where(low, one, two).astype(jnp.bfloat16)
    own_rows.wait()
    alive = lax.broadcasted_iota(jnp.int32, (rows, wide), 0) + rank * rows < fresh
    for step in range(steps):
        columns = slice(step * wide, (step + 1) * wide)
        loads[step].wait()
        mixed = jnp.dot(joined[...], w_out[step], preferred_element_type=jnp.float32)
        value = hidden[:, columns].astype(jnp.float32) + mixed
        result[:, columns] = jnp.where(alive, value, 0.0).astype(jnp.bfloat16)
    for move in moves:
        move.wait()


def finish(scalars, heads, w_out, hidden_in, received):
    model = w_out.shape[1]
    vector = pl.BlockSpec(memory_space=pltpu.VMEM)
    far = pl.BlockSpec(memory_space=pltpu.HBM)
    return pl.pallas_call(
        finish_kernel,
        out_shape=(
            jax.ShapeDtypeStruct((PART_ROWS, model), jnp.bfloat16),
            jax.ShapeDtypeStruct(received.shape, received.dtype),
        ),
        in_specs=[pl.BlockSpec(memory_space=pltpu.SMEM), vector, far, far, far],
        out_specs=[vector, far],
        scratch_shapes=[
            pltpu.VMEM((model // FINISH_COLUMNS, w_out.shape[0], FINISH_COLUMNS), jnp.bfloat16),
            pltpu.VMEM((PART_ROWS, model), jnp.bfloat16),
            pltpu.VMEM((PART_ROWS, w_out.shape[0]), jnp.bfloat16),
            pltpu.SemaphoreType.DMA((model // FINISH_COLUMNS + 1,)),
            pltpu.SemaphoreType.DMA((received.shape[0] // 8,)),
        ],
        compiler_params=pltpu.CompilerParams(vmem_limit_bytes=57 * MIB),
        cost_estimate=pl.CostEstimate(
            flops=2 * PART_ROWS * w_out.shape[0] * model,
            bytes_accessed=12 * MIB,
            transcendentals=0,
        ),
        name="finish",
    )(scalars, heads, w_out, hidden_in, received)


def shards(
    hidden_in,
    norm_gain,
    w_query,
    key_value_weight,
    w_out,
    prior_cache,
    cache_len,
    group_len,
    page_map,
):
    rank = lax.axis_index("tp").astype(jnp.int32)
    tp_count = lax.axis_size("tp")
    req_count = lax.axis_size("req")
    scalars = jnp.stack([cache_len[0], group_len[0], rank])

    half_size = HEAD_SIZE // 2
    frequency = 10000.0 ** (-(jnp.arange(half_size, dtype=jnp.float32) * 2.0 / HEAD_SIZE))
    positions = cache_len[0] + jnp.arange(NEW_TOKEN_SLOTS, dtype=jnp.int32)
    angles = positions.astype(jnp.float32)[:, None] * jnp.tile(frequency, 4)[None, :]
    sign = jnp.where(jnp.arange(LANES) % HEAD_SIZE < half_size, -1.0, 1.0)
    cosine = jnp.cos(angles)
    sine = jnp.sin(angles) * sign[None, :]

    targets = jnp.arange(req_count, dtype=jnp.int32) * tp_count + rank
    order = jnp.arange(page_map.shape[1], dtype=jnp.int32)
    picks = jnp.sum(
        jnp.where(page_map[0][None, :] == targets[:, None], order[None, :], 0), axis=1
    ).astype(jnp.int32)

    prior = prior_cache[0]
    queries, keyval = project(hidden_in, norm_gain, w_query, key_value_weight, cosine, sine)
    outgoing = pick_blocks(scalars, picks, prior, keyval)
    outgoing, scalars = lax.optimization_barrier((outgoing, scalars))
    received = lax.all_to_all(outgoing, "req", split_axis=0, concat_axis=0, tiled=True)
    attended = attend(scalars, queries, prior, keyval)
    attended, received = lax.optimization_barrier((attended, received))
    heads = lax.all_to_all(attended, "tp", split_axis=0, concat_axis=0, tiled=True)
    hidden_out, decode_kv = finish(scalars, heads, w_out, hidden_in, received)
    return (hidden_out, decode_kv[None])


def solution(mesh):
    placed = (
        P("req", None),
        P(),
        P(None, "tp"),
        P(),
        P(),
        P("req", None, None),
        P("req"),
        P("req"),
        P("req", None),
    )
    return jax.shard_map(
        shards,
        mesh=mesh,
        in_specs=placed,
        out_specs=(P(("req", "tp"), None), P(("req", "tp"), None, None, None)),
        check_vma=False,
    )
```

```python
import jax
import jax.numpy as jnp
import numpy as np
from jax import lax
from jax.experimental import pallas as pl
from jax.experimental.pallas import tpu as pltpu
from jax.sharding import PartitionSpec as P

QUERY_HEAD_COUNT = 20
KEY_VALUE_HEADS = 5
HEAD_SIZE = 64
GROUP = QUERY_HEAD_COUNT // KEY_VALUE_HEADS
NEW_TOKEN_SLOTS = 1024
PRIOR_SLOTS = 7168
SPAN = KEY_VALUE_HEADS * HEAD_SIZE
WIDTH = 2 * SPAN
LANES = 128
WINDOW = 256
LOCAL = 5
TP = QUERY_HEAD_COUNT // LOCAL
QUERY_ROWS = 512
QUERY_BLOCKS = NEW_TOKEN_SLOTS // QUERY_ROWS
STACK = LOCAL * QUERY_ROWS
KEY_ROWS = 1024
PREPARE_ROWS = 256
PROJECT_ROWS = 512
NORM_ROWS = 256
PART_ROWS = 256
FINISH_COLUMNS = 512
PACKED = PART_ROWS * LOCAL // 2
BLOCK_ROWS = 64
MIB = 1 << 20


def lane_ids(rows):
    return lax.broadcasted_iota(jnp.int32, (rows, LANES), 1)


def local_kv(rank, head):
    return (rank * LOCAL + head) // GROUP - rank


def key_tile_start(rank):
    return rank // 2


def value_tile_start(rank):
    return jnp.where(rank == 0, 2, 3)


def key_offset(rank):
    return rank * HEAD_SIZE - key_tile_start(rank) * LANES


def value_offset(rank):
    return SPAN + rank * HEAD_SIZE - value_tile_start(rank) * LANES


def rotate(tile, cosine, sine):
    low = lane_ids(tile.shape[0]) % HEAD_SIZE < HEAD_SIZE // 2
    half = HEAD_SIZE // 2
    other = jnp.where(low, pltpu.roll(tile, LANES - half, 1), pltpu.roll(tile, half, 1))
    return tile * cosine + other * sine


def project_kernel(
    cache_len,
    group_len,
    page_map,
    hidden_hbm,
    gain,
    w_query_hbm,
    w_keyval_hbm,
    frequency,
    prior,
    queries,
    keyval,
    outgoing,
    hidden,
    w_query,
    w_keyval,
    normed,
    mixed_q,
    mixed_kv,
    cosine,
    sine,
    semaphores,
    block_semaphores,
):
    cached, fresh = cache_len[0], group_len[0]
    rank = lax.axis_index("tp")
    total = hidden.shape[0]
    pieces = total // NORM_ROWS
    loads = [
        pltpu.make_async_copy(
            hidden_hbm.at[pl.ds(piece * NORM_ROWS, NORM_ROWS)],
            hidden.at[pl.ds(piece * NORM_ROWS, NORM_ROWS)],
            semaphores.at[piece],
        )
        for piece in range(pieces)
    ]
    weights = [
        pltpu.make_async_copy(w_keyval_hbm, w_keyval, semaphores.at[pieces]),
        pltpu.make_async_copy(w_query_hbm, w_query, semaphores.at[pieces + 1]),
    ]
    for copy in loads[:2] + weights + loads[2:]:
        copy.start()

    def prior_copy(block, slot):
        start = pl.multiple_of(block * BLOCK_ROWS, BLOCK_ROWS)
        return pltpu.make_async_copy(
            prior.at[pl.ds(start, BLOCK_ROWS)], outgoing.at[slot], block_semaphores.at[slot]
        )

    def send(block, carry):
        device = page_map[0, block]
        slot = device // TP
        ours = device % TP == rank

        @pl.when(ours & (block * BLOCK_ROWS < cached))
        def _():
            prior_copy(block, slot).start()

        @pl.when(ours & (block * BLOCK_ROWS >= cached))
        def _():
            outgoing[slot] = jnp.zeros((BLOCK_ROWS, WIDTH), jnp.bfloat16)

        return carry

    lax.fori_loop(0, PRIOR_SLOTS // BLOCK_ROWS, send, 0)

    count = 32
    steps = lax.broadcasted_iota(jnp.int32, (count, LANES), 0)
    coarse = (steps * count + cached).astype(jnp.float32) * frequency[...]
    fine = steps.astype(jnp.float32) * frequency[...]
    coarse_cos, coarse_sin = jnp.cos(coarse), jnp.sin(coarse)
    fine_cos, fine_sin = jnp.cos(fine), jnp.sin(fine)
    low_half = lane_ids(count) % HEAD_SIZE < HEAD_SIZE // 2
    for step in range(total // count):
        here = pl.ds(step * count, count)
        far_cos, far_sin = coarse_cos[step : step + 1], coarse_sin[step : step + 1]
        cosine[here] = far_cos * fine_cos - far_sin * fine_sin
        both = far_sin * fine_cos + far_cos * fine_sin
        sine[here] = jnp.where(low_half, -both, both)

    def norm(piece):
        here = pl.ds(piece * NORM_ROWS, NORM_ROWS)
        value = hidden[here].astype(jnp.float32)
        scale = lax.rsqrt(jnp.mean(value * value, axis=-1, keepdims=True) + 1e-05)
        normed[here] = (value * scale * scale_row).astype(jnp.bfloat16)

    scale_row = gain[...].astype(jnp.float32).reshape(1, -1)
    lanes = lane_ids(PROJECT_ROWS)

    def mix(block):
        here = pl.ds(block * PROJECT_ROWS, PROJECT_ROWS)
        rows = normed[here]
        mixed_kv[here] = jnp.dot(rows, w_keyval[...], preferred_element_type=jnp.float32)
        mixed_q[here, :SPAN] = lax.dot_general(
            rows, w_query[...], (((1,), (1,)), ((), ())), preferred_element_type=jnp.float32
        )

    def turn(block):
        here = pl.ds(block * PROJECT_ROWS, PROJECT_ROWS)
        cos, sin = cosine[here], sine[here]
        for tile in range(WIDTH // LANES):
            columns = slice(tile * LANES, (tile + 1) * LANES)
            raw = mixed_kv[here, columns]
            if tile < 2:
                raw = rotate(raw, cos, sin)
            elif tile == 2:
                raw = jnp.where(lanes < HEAD_SIZE, rotate(raw, cos, sin), raw)
            keyval[here, columns] = raw.astype(jnp.bfloat16)
        for tile in range(3):
            raw = mixed_q[here, tile * LANES : (tile + 1) * LANES]
            turned = rotate(raw, cos, sin) * HEAD_SIZE**-0.5
            for head in range(2 * tile, min(2 * tile + 2, LOCAL)):
                own = turned if head % 2 == 0 else pltpu.roll(turned, HEAD_SIZE, 1)
                queries[block, head * QUERY_ROWS : (head + 1) * QUERY_ROWS] = own[
                    :, :HEAD_SIZE
                ].astype(jnp.bfloat16)

    for piece in range(2):
        loads[piece].wait()
        norm(piece)
    for copy in weights + loads[2:]:
        copy.wait()
    mix(0)
    norm(2)
    norm(3)
    mix(1)
    turn(0)
    turn(1)

    def trim(slot, live, value):
        rows = lax.broadcasted_iota(jnp.int32, (BLOCK_ROWS, WIDTH), 0)
        outgoing[slot] = jnp.where(rows < live, value.astype(jnp.float32), 0.0).astype(jnp.bfloat16)

    for block in range(total // BLOCK_ROWS):
        device = page_map[0, PRIOR_SLOTS // BLOCK_ROWS + block]

        @pl.when(device % TP == rank)
        def _():
            trim(device // TP, fresh - block * BLOCK_ROWS, keyval[pl.ds(block * BLOCK_ROWS, BLOCK_ROWS)])

    def receive(block, carry):
        device = page_map[0, block]
        slot = device // TP
        live = cached - block * BLOCK_ROWS
        ours = (device % TP == rank) & (live > 0)

        @pl.when(ours)
        def _():
            prior_copy(block, slot).wait()

        @pl.when(ours & (live < BLOCK_ROWS))
        def _():
            trim(slot, live, outgoing[slot])

        return carry

    lax.fori_loop(0, PRIOR_SLOTS // BLOCK_ROWS, receive, 0)


def project(cache_len, group_len, page_map, hidden_in, norm_gain, w_query, w_keyval, prior):
    rows, model = hidden_in.shape
    half_size = HEAD_SIZE // 2
    frequency = 10000.0 ** (-(np.arange(half_size, dtype=np.float64) * 2.0 / HEAD_SIZE))
    frequency = jnp.asarray(np.tile(frequency, LANES // half_size)[None].astype(np.float32))
    count = page_map.shape[1] // TP
    scalar = pl.BlockSpec(memory_space=pltpu.SMEM)
    vector = pl.BlockSpec(memory_space=pltpu.VMEM)
    far = pl.BlockSpec(memory_space=pltpu.HBM)
    return pl.pallas_call(
        project_kernel,
        out_shape=(
            jax.ShapeDtypeStruct((QUERY_BLOCKS, STACK, HEAD_SIZE), jnp.bfloat16),
            jax.ShapeDtypeStruct((rows, WIDTH), jnp.bfloat16),
            jax.ShapeDtypeStruct((count, BLOCK_ROWS, WIDTH), jnp.bfloat16),
        ),
        in_specs=[scalar, scalar, scalar, far, vector, far, far, vector, far],
        out_specs=[vector, vector, vector],
        scratch_shapes=[
            pltpu.VMEM((rows, model), jnp.bfloat16),
            pltpu.VMEM((SPAN, model), jnp.bfloat16),
            pltpu.VMEM((model, WIDTH), jnp.bfloat16),
            pltpu.VMEM((rows, model), jnp.bfloat16),
            pltpu.VMEM((rows, 3 * LANES), jnp.float32),
            pltpu.VMEM((rows, WIDTH), jnp.float32),
            pltpu.VMEM((rows, LANES), jnp.float32),
            pltpu.VMEM((rows, LANES), jnp.float32),
            pltpu.SemaphoreType.DMA((rows // NORM_ROWS + 2,)),
            pltpu.SemaphoreType.DMA((count,)),
        ],
        compiler_params=pltpu.CompilerParams(vmem_limit_bytes=58 * MIB),
        cost_estimate=pl.CostEstimate(
            flops=2 * rows * model * (SPAN + WIDTH), bytes_accessed=15 * MIB, transcendentals=0
        ),
        name="project",
    )(
        cache_len,
        group_len,
        page_map,
        hidden_in,
        norm_gain,
        w_query.T,
        w_keyval,
        frequency,
        prior,
    )


def attend_kernel(
    cache_len,
    group_len,
    queries,
    prior,
    fresh_rows,
    heads_out,
    raw_keys,
    raw_values,
    keys,
    values,
    top,
    total,
    semaphores,
):
    cached, fresh, rank = cache_len[0], group_len[0], lax.axis_index("tp")
    key_start = pl.multiple_of(key_tile_start(rank) * LANES, LANES)
    value_start = pl.multiple_of(value_tile_start(rank) * LANES, LANES)
    key_shift, value_shift = key_offset(rank), value_offset(rank)
    prior_chunks = (cached + KEY_ROWS - 1) // KEY_ROWS
    blocks = (fresh + QUERY_ROWS - 1) // QUERY_ROWS
    chunk_limit = PRIOR_SLOTS // KEY_ROWS

    def copies(chunk):
        into = pl.ds(chunk * KEY_ROWS, KEY_ROWS)
        return (
            pltpu.make_async_copy(
                prior.at[into, pl.ds(key_start, WINDOW)],
                raw_keys.at[into],
                semaphores.at[0, chunk],
            ),
            pltpu.make_async_copy(
                prior.at[into, pl.ds(value_start, WINDOW)],
                raw_values.at[into],
                semaphores.at[1, chunk],
            ),
        )

    into = pl.ds(PRIOR_SLOTS, NEW_TOKEN_SLOTS)
    fresh_copies = (
        pltpu.make_async_copy(
            fresh_rows.at[:, pl.ds(key_start, WINDOW)],
            raw_keys.at[into],
            semaphores.at[0, chunk_limit],
        ),
        pltpu.make_async_copy(
            fresh_rows.at[:, pl.ds(value_start, WINDOW)],
            raw_values.at[into],
            semaphores.at[1, chunk_limit],
        ),
    )
    for copy in fresh_copies:
        copy.start()
    for chunk in range(chunk_limit):

        @pl.when(chunk < prior_chunks)
        def _():
            for copy in copies(chunk):
                copy.start()

    def prepare(start, live):
        here = pl.ds(start, PREPARE_ROWS)
        lanes = lane_ids(PREPARE_ROWS)
        alive = lax.broadcasted_iota(jnp.int32, (PREPARE_ROWS, LANES), 0) < live
        raw = raw_keys[here].astype(jnp.float32)
        low, high = raw[:, :LANES], raw[:, LANES:]
        spare = raw_keys[0:8].astype(jnp.float32)[0:1]
        low = jnp.where(alive, low, spare[:, :LANES])
        high = jnp.where(alive, high, spare[:, LANES:])
        joined = jnp.where(
            lanes < HEAD_SIZE, pltpu.roll(low, HEAD_SIZE, 1), pltpu.roll(high, HEAD_SIZE, 1)
        )
        pair = jnp.where(key_shift == 0, low, joined)
        keys[:, here] = pair.T.astype(jnp.bfloat16)
        raw = raw_values[here].astype(jnp.float32)
        low, high = raw[:, :LANES], raw[:, LANES:]
        low_turned, high_turned = pltpu.roll(low, HEAD_SIZE, 1), pltpu.roll(high, HEAD_SIZE, 1)
        one = jnp.where(
            value_shift == 0, low, jnp.where(value_shift == HEAD_SIZE, low_turned, high)
        )
        two = jnp.where(
            value_shift == 0, low_turned, jnp.where(value_shift == HEAD_SIZE, high, high_turned)
        )
        for slot, own in enumerate((one, two)):
            own = jnp.where(alive, jnp.where(lanes < HEAD_SIZE, own, 1.0), 0.0)
            values[slot, here] = own.astype(jnp.bfloat16)

    def score(block, head, start, rows):
        which = local_kv(rank, head)
        return jnp.dot(
            queries[block, head * QUERY_ROWS : (head + 1) * QUERY_ROWS],
            keys[pl.ds(pl.multiple_of(which * HEAD_SIZE, HEAD_SIZE), HEAD_SIZE), pl.ds(start, rows)],
            preferred_element_type=jnp.float32,
        )

    def blend(head, start, rows, scores, masked):
        own = slice(head * QUERY_ROWS, (head + 1) * QUERY_ROWS)
        if masked:
            row = lax.broadcasted_iota(jnp.int32, scores.shape, 0)
            column = lax.broadcasted_iota(jnp.int32, scores.shape, 1)
            scores = jnp.where(column <= row, scores, -1e30)
        before = top[own]
        after = jnp.maximum(before, jnp.max(scores, axis=-1, keepdims=True))
        rescale = jnp.exp(before - after)
        chances = jnp.exp(scores - jnp.tile(after, (1, rows // LANES))).astype(jnp.bfloat16)
        top[own] = after
        total[own] = total[own] * rescale + jnp.dot(
            chances,
            values[local_kv(rank, head), pl.ds(start, rows)],
            preferred_element_type=jnp.float32,
        )

    def absorb(block, start, rows, masked):
        pending = score(block, 0, start, rows)
        for head in range(LOCAL):
            following = score(block, head + 1, start, rows) if head + 1 < LOCAL else None
            blend(head, start, rows, pending, masked)
            pending = following

    def query_block(block, carry):
        top[...] = jnp.full_like(top, -1e30)
        total[...] = jnp.zeros_like(total)

        @pl.when(block == 0)
        def _():
            for copy in fresh_copies:
                copy.wait()

            def each(step, inner):
                start = pl.multiple_of(PRIOR_SLOTS + step * PREPARE_ROWS, PREPARE_ROWS)
                prepare(start, PREPARE_ROWS)
                return inner

            lax.fori_loop(0, NEW_TOKEN_SLOTS // PREPARE_ROWS, each, 0)

        def earlier(step, inner):
            start = pl.multiple_of(PRIOR_SLOTS + step * QUERY_ROWS, QUERY_ROWS)
            absorb(block, start, QUERY_ROWS, False)
            return inner

        def cache(step, inner):
            start = pl.multiple_of(step * KEY_ROWS, KEY_ROWS)

            @pl.when(block == 0)
            def _():
                for copy in copies(step):
                    copy.wait()

                def each(part, most):
                    here = pl.multiple_of(start + part * PREPARE_ROWS, PREPARE_ROWS)
                    prepare(here, cached - here)
                    return most

                lax.fori_loop(0, KEY_ROWS // PREPARE_ROWS, each, 0)

            absorb(block, start, KEY_ROWS, False)
            return inner

        start = pl.multiple_of(PRIOR_SLOTS + block * QUERY_ROWS, QUERY_ROWS)
        absorb(block, start, QUERY_ROWS, True)
        lax.fori_loop(0, block, earlier, 0)
        lax.fori_loop(0, prior_chunks, cache, 0)

        lanes = lane_ids(QUERY_ROWS)
        odd = rank % 2 == 1
        plain, turned = [], []
        for head in range(LOCAL):
            sums = total[head * QUERY_ROWS : (head + 1) * QUERY_ROWS]
            swapped = pltpu.roll(sums, HEAD_SIZE, 1)
            plain.append(sums / swapped)
            turned.append(swapped / sums)
        even_pairs = [jnp.where(lanes < HEAD_SIZE, plain[i], turned[i + 1]) for i in (0, 2)]
        odd_pairs = [jnp.where(lanes < HEAD_SIZE, plain[i], turned[i + 1]) for i in (1, 3)]
        single = jnp.where(odd, plain[0], plain[4])
        single_turned = jnp.where(odd, turned[0], turned[4])
        near = (lane_ids(LANES) < HEAD_SIZE) != odd
        for part in range(QUERY_ROWS // PART_ROWS):
            slot = block * (QUERY_ROWS // PART_ROWS) + part
            rows = slice(part * PART_ROWS, (part + 1) * PART_ROWS)
            for tile in range(2):
                pair = jnp.where(odd, odd_pairs[tile][rows], even_pairs[tile][rows])
                heads_out[slot, tile * PART_ROWS : (tile + 1) * PART_ROWS] = pair.astype(
                    jnp.bfloat16
                )
            begin = part * PART_ROWS
            above, below = slice(begin, begin + LANES), slice(begin + LANES, begin + PART_ROWS)
            packed = jnp.where(
                odd,
                jnp.where(near, single_turned[above], single[below]),
                jnp.where(near, single[above], single_turned[below]),
            )
            heads_out[slot, 2 * PART_ROWS :] = packed.astype(jnp.bfloat16)
        return carry

    lax.fori_loop(0, blocks, query_block, 0)

    def idle(slot, carry):
        heads_out[slot] = jnp.zeros((PACKED, LANES), jnp.bfloat16)
        return carry

    parts = QUERY_ROWS // PART_ROWS
    lax.fori_loop(blocks * parts, QUERY_BLOCKS * parts, idle, 0)


def attend(cache_len, group_len, queries, prior, fresh_rows):
    context = PRIOR_SLOTS + NEW_TOKEN_SLOTS
    vector = pl.BlockSpec(memory_space=pltpu.VMEM)
    return pl.pallas_call(
        attend_kernel,
        out_shape=jax.ShapeDtypeStruct(
            (NEW_TOKEN_SLOTS // PART_ROWS, PACKED, LANES), jnp.bfloat16
        ),
        in_specs=[
            pl.BlockSpec(memory_space=pltpu.SMEM),
            pl.BlockSpec(memory_space=pltpu.SMEM),
            vector,
            pl.BlockSpec(memory_space=pltpu.HBM),
            pl.BlockSpec(memory_space=pl.ANY),
        ],
        out_specs=vector,
        scratch_shapes=[
            pltpu.VMEM((context, WINDOW), jnp.bfloat16),
            pltpu.VMEM((context, WINDOW), jnp.bfloat16),
            pltpu.VMEM((LANES, context), jnp.bfloat16),
            pltpu.VMEM((2, context, LANES), jnp.bfloat16),
            pltpu.VMEM((STACK, LANES), jnp.float32),
            pltpu.VMEM((STACK, LANES), jnp.float32),
            pltpu.SemaphoreType.DMA((2, PRIOR_SLOTS // KEY_ROWS + 1)),
        ],
        compiler_params=pltpu.CompilerParams(vmem_limit_bytes=56 * MIB),
        cost_estimate=pl.CostEstimate(
            flops=4 * 5120 * 7680 * 256, bytes_accessed=12 * MIB, transcendentals=5120 * 7680
        ),
        name="attend",
    )(cache_len, group_len, queries, prior, fresh_rows)


def finish_kernel(
    group_len,
    heads,
    w_out_hbm,
    hidden_hbm,
    received,
    result,
    decode,
    w_out,
    hidden,
    joined,
    passing,
    semaphores,
    move_semaphores,
):
    rank, fresh = lax.axis_index("tp"), group_len[0]
    rows = result.shape[0]
    wide = FINISH_COLUMNS
    steps = result.shape[1] // wide
    loads = [
        pltpu.make_async_copy(
            w_out_hbm.at[:, pl.ds(step * wide, wide)], w_out.at[step], semaphores.at[step]
        )
        for step in range(steps)
    ]
    own_rows = pltpu.make_async_copy(
        hidden_hbm.at[pl.ds(pl.multiple_of(rank * rows, rows), rows)], hidden, semaphores.at[steps]
    )
    for copy in loads[:1] + [own_rows] + loads[1:]:
        copy.start()
    pieces = move_semaphores.shape[1]
    slots = received.shape[0] // pieces
    fetches, stores = [], []
    for piece in range(pieces):
        here = pl.ds(piece * slots, slots)
        fetches.append(
            pltpu.make_async_copy(received.at[here], passing.at[here], move_semaphores.at[0, piece])
        )
        stores.append(
            pltpu.make_async_copy(passing.at[here], decode.at[here], move_semaphores.at[1, piece])
        )
    for copy in fetches:
        copy.start()
    low = lane_ids(LANES) < HEAD_SIZE
    for pair in range(2):
        first, second = heads.at[2 * pair], heads.at[2 * pair + 1]
        for tile in range(2):
            source = slice(tile * PART_ROWS, (tile + 1) * PART_ROWS)
            columns = (5 * pair + tile) * LANES
            joined[:, columns : columns + LANES] = first[source]
            joined[:, columns + 3 * LANES : columns + 4 * LANES] = second[source]
        one = first[2 * PART_ROWS :].astype(jnp.float32)
        two = second[2 * PART_ROWS :].astype(jnp.float32)
        columns = (5 * pair + 2) * LANES
        joined[:LANES, columns : columns + LANES] = jnp.where(low, one, two).astype(jnp.bfloat16)
        one, two = pltpu.roll(one, HEAD_SIZE, 1), pltpu.roll(two, HEAD_SIZE, 1)
        joined[LANES:, columns : columns + LANES] = jnp.where(low, one, two).astype(jnp.bfloat16)
    for fetch, store in zip(fetches, stores):
        fetch.wait()
        store.start()
    own_rows.wait()
    alive = lax.broadcasted_iota(jnp.int32, (rows, wide), 0) + rank * rows < fresh
    for step in range(steps):
        columns = slice(step * wide, (step + 1) * wide)
        loads[step].wait()
        mixed = jnp.dot(joined[...], w_out[step], preferred_element_type=jnp.float32)
        value = hidden[:, columns].astype(jnp.float32) + mixed
        result[:, columns] = jnp.where(alive, value, 0.0).astype(jnp.bfloat16)
    for store in stores:
        store.wait()


def finish(group_len, heads, w_out, hidden_in, received):
    model = w_out.shape[1]
    vector = pl.BlockSpec(memory_space=pltpu.VMEM)
    far = pl.BlockSpec(memory_space=pltpu.HBM)
    return pl.pallas_call(
        finish_kernel,
        out_shape=(
            jax.ShapeDtypeStruct((PART_ROWS, model), jnp.bfloat16),
            jax.ShapeDtypeStruct(received.shape, received.dtype),
        ),
        in_specs=[pl.BlockSpec(memory_space=pltpu.SMEM), vector, far, far, far],
        out_specs=[vector, far],
        scratch_shapes=[
            pltpu.VMEM((model // FINISH_COLUMNS, w_out.shape[0], FINISH_COLUMNS), jnp.bfloat16),
            pltpu.VMEM((PART_ROWS, model), jnp.bfloat16),
            pltpu.VMEM((PART_ROWS, w_out.shape[0]), jnp.bfloat16),
            pltpu.VMEM(received.shape, received.dtype),
            pltpu.SemaphoreType.DMA((model // FINISH_COLUMNS + 1,)),
            pltpu.SemaphoreType.DMA((2, 4)),
        ],
        compiler_params=pltpu.CompilerParams(vmem_limit_bytes=58 * MIB),
        cost_estimate=pl.CostEstimate(
            flops=2 * PART_ROWS * w_out.shape[0] * model,
            bytes_accessed=12 * MIB,
            transcendentals=0,
        ),
        name="finish",
    )(group_len, heads, w_out, hidden_in, received)


def shards(
    hidden_in,
    norm_gain,
    w_query,
    key_value_weight,
    w_out,
    prior_cache,
    cache_len,
    group_len,
    page_map,
):
    prior = prior_cache[0]
    queries, keyval, outgoing = project(
        cache_len, group_len, page_map, hidden_in, norm_gain, w_query, key_value_weight, prior
    )
    outgoing, queries = lax.optimization_barrier((outgoing, queries))
    received = lax.all_to_all(outgoing, "req", split_axis=0, concat_axis=0, tiled=True)
    attended = attend(cache_len, group_len, queries, prior, keyval)
    attended, received = lax.optimization_barrier((attended, received))
    heads = lax.all_to_all(attended, "tp", split_axis=0, concat_axis=0, tiled=True)
    hidden_out, decode_kv = finish(group_len, heads, w_out, hidden_in, received)
    return (hidden_out, decode_kv[None])


def solution(mesh):
    placed = (
        P("req", None),
        P(),
        P(None, "tp"),
        P(),
        P(),
        P("req", None, None),
        P("req"),
        P("req"),
        P("req", None),
    )
    return jax.shard_map(
        shards,
        mesh=mesh,
        in_specs=placed,
        out_specs=(P(("req", "tp"), None), P(("req", "tp"), None, None, None)),
        check_vma=False,
    )
```

```python
import jax
import jax.numpy as jnp
import numpy as np
from jax import lax
from jax.experimental import pallas as pl
from jax.experimental.pallas import tpu as pltpu
from jax.sharding import PartitionSpec as P

QUERY_HEAD_COUNT = 20
KEY_VALUE_HEADS = 5
HEAD_SIZE = 64
GROUP = QUERY_HEAD_COUNT // KEY_VALUE_HEADS
NEW_TOKEN_SLOTS = 1024
PRIOR_SLOTS = 7168
SPAN = KEY_VALUE_HEADS * HEAD_SIZE
WIDTH = 2 * SPAN
LANES = 128
WINDOW = 256
LOCAL = 5
TP = QUERY_HEAD_COUNT // LOCAL
TP_BITS = TP.bit_length() - 1
KEPT = 1 << 20
QUERY_ROWS = 512
QUERY_BLOCKS = NEW_TOKEN_SLOTS // QUERY_ROWS
STACK = LOCAL * QUERY_ROWS
KEY_ROWS = 1792
PREPARE_ROWS = 256
PROJECT_ROWS = 512
NORM_ROWS = 256
PART_ROWS = 256
FINISH_COLUMNS = 512
FINISH_LIMIT = 24
STORE_LIMIT = 24
PACKED = PART_ROWS * LOCAL // 2
BLOCK_ROWS = 64
MIB = 1 << 20


def lane_ids(rows):
    return lax.broadcasted_iota(jnp.int32, (rows, LANES), 1)


def local_kv(rank, head):
    return (rank * LOCAL + head) // GROUP - rank


def key_tile_start(rank):
    return rank // 2


def value_tile_start(rank):
    return jnp.where(rank == 0, 2, 3)


def key_offset(rank):
    return rank * HEAD_SIZE - key_tile_start(rank) * LANES


def value_offset(rank):
    return SPAN + rank * HEAD_SIZE - value_tile_start(rank) * LANES


def rotate(tile, cosine, sine):
    low = lane_ids(tile.shape[0]) % HEAD_SIZE < HEAD_SIZE // 2
    half = HEAD_SIZE // 2
    other = jnp.where(low, pltpu.roll(tile, LANES - half, 1), pltpu.roll(tile, half, 1))
    return tile * cosine + other * sine


def project_kernel(
    cache_len,
    group_len,
    page_map,
    hidden_hbm,
    gain,
    w_query_hbm,
    w_keyval_hbm,
    frequency,
    prior,
    queries_hbm,
    keyval_hbm,
    outgoing_hbm,
    queries,
    keyval,
    outgoing,
    live_rows,
    hidden,
    w_query,
    w_keyval,
    normed,
    mixed_q,
    mixed_kv,
    cosine,
    sine,
    semaphores,
    block_semaphores,
    store_semaphores,
    result_semaphores,
):
    cached, fresh = cache_len[0], group_len[0]
    rank = lax.axis_index("tp")
    total = hidden.shape[0]
    pieces = total // NORM_ROWS
    loads = [
        pltpu.make_async_copy(
            hidden_hbm.at[pl.ds(piece * NORM_ROWS, NORM_ROWS)],
            hidden.at[pl.ds(piece * NORM_ROWS, NORM_ROWS)],
            semaphores.at[piece],
        )
        for piece in range(pieces)
    ]
    weights = [
        pltpu.make_async_copy(w_keyval_hbm, w_keyval, semaphores.at[pieces]),
        pltpu.make_async_copy(w_query_hbm, w_query, semaphores.at[pieces + 1]),
    ]
    for copy in loads[:2] + weights + loads[2:]:
        copy.start()

    def prior_copy(block, slot):
        start = pl.multiple_of(block * BLOCK_ROWS, BLOCK_ROWS)
        return pltpu.make_async_copy(
            prior.at[pl.ds(start, BLOCK_ROWS)], outgoing.at[slot], block_semaphores.at[slot]
        )

    def block_store(slot):
        return pltpu.make_async_copy(
            outgoing.at[slot], outgoing_hbm.at[slot], store_semaphores.at[slot]
        )

    def send(block, carry):
        device = page_map[0, block]

        @pl.when(device & (TP - 1) == rank)
        def _():
            slot = device >> TP_BITS
            live = cached - block * BLOCK_ROWS
            live_rows[slot] = live

            @pl.when(live > 0)
            def _():
                prior_copy(block, slot).start()

        return carry

    prior_blocks = PRIOR_SLOTS // BLOCK_ROWS
    lax.fori_loop(0, prior_blocks, send, 0, unroll=8)
    for block in range(total // BLOCK_ROWS):
        device = page_map[0, prior_blocks + block]

        @pl.when(device & (TP - 1) == rank)
        def _():
            live_rows[device >> TP_BITS] = KEPT

    count = 32
    steps = lax.broadcasted_iota(jnp.int32, (count, LANES), 0)
    coarse = (steps * count + cached).astype(jnp.float32) * frequency[...]
    fine = steps.astype(jnp.float32) * frequency[...]
    coarse_cos, coarse_sin = jnp.cos(coarse), jnp.sin(coarse)
    fine_cos, fine_sin = jnp.cos(fine), jnp.sin(fine)
    low_half = lane_ids(count) % HEAD_SIZE < HEAD_SIZE // 2
    for step in range(total // count):
        here = pl.ds(step * count, count)
        far_cos, far_sin = coarse_cos[step : step + 1], coarse_sin[step : step + 1]
        cosine[here] = far_cos * fine_cos - far_sin * fine_sin
        both = far_sin * fine_cos + far_cos * fine_sin
        sine[here] = jnp.where(low_half, -both, both)

    def norm(piece):
        here = pl.ds(piece * NORM_ROWS, NORM_ROWS)
        value = hidden[here].astype(jnp.float32)
        scale = lax.rsqrt(jnp.mean(value * value, axis=-1, keepdims=True) + 1e-05)
        normed[here] = (value * scale * scale_row).astype(jnp.bfloat16)

    scale_row = gain[...].astype(jnp.float32).reshape(1, -1)
    lanes = lane_ids(PROJECT_ROWS)

    def mix(block):
        here = pl.ds(block * PROJECT_ROWS, PROJECT_ROWS)
        rows = normed[here]
        mixed_kv[here] = jnp.dot(rows, w_keyval[...], preferred_element_type=jnp.float32)
        mixed_q[here, :SPAN] = lax.dot_general(
            rows, w_query[...], (((1,), (1,)), ((), ())), preferred_element_type=jnp.float32
        )

    def turn(block):
        here = pl.ds(block * PROJECT_ROWS, PROJECT_ROWS)
        cos, sin = cosine[here], sine[here]
        for tile in range(WIDTH // LANES):
            columns = slice(tile * LANES, (tile + 1) * LANES)
            raw = mixed_kv[here, columns]
            if tile < 2:
                raw = rotate(raw, cos, sin)
            elif tile == 2:
                raw = jnp.where(lanes < HEAD_SIZE, rotate(raw, cos, sin), raw)
            keyval[here, columns] = raw.astype(jnp.bfloat16)
        for tile in range(3):
            raw = mixed_q[here, tile * LANES : (tile + 1) * LANES]
            turned = rotate(raw, cos, sin) * HEAD_SIZE**-0.5
            for head in range(2 * tile, min(2 * tile + 2, LOCAL)):
                own = turned if head % 2 == 0 else pltpu.roll(turned, HEAD_SIZE, 1)
                queries[block, head * QUERY_ROWS : (head + 1) * QUERY_ROWS] = own[
                    :, :HEAD_SIZE
                ].astype(jnp.bfloat16)

    def trim(slot, live, value):
        rows = lax.broadcasted_iota(jnp.int32, (BLOCK_ROWS, WIDTH), 0)
        outgoing[slot] = jnp.where(rows < live, value.astype(jnp.float32), 0.0).astype(jnp.bfloat16)

    def forward(slot, carry):
        live = live_rows[slot]

        @pl.when((live > 0) & (live < KEPT))
        def _():
            prior_copy(0, slot).wait()

        @pl.when((live > 0) & (live < BLOCK_ROWS))
        def _():
            trim(slot, live, outgoing[slot])

        @pl.when(live <= 0)
        def _():
            outgoing[slot] = jnp.zeros((BLOCK_ROWS, WIDTH), jnp.bfloat16)

        @pl.when(live < KEPT)
        def _():
            block_store(slot).start()

        return carry

    def result_stores(block):
        here = pl.ds(block * PROJECT_ROWS, PROJECT_ROWS)
        return [
            pltpu.make_async_copy(
                keyval.at[here], keyval_hbm.at[here], result_semaphores.at[0, block]
            ),
            pltpu.make_async_copy(
                queries.at[block], queries_hbm.at[block], result_semaphores.at[1, block]
            ),
        ]

    for piece in range(2):
        loads[piece].wait()
        norm(piece)
    for copy in weights + loads[2:]:
        copy.wait()
    mix(0)
    norm(2)
    norm(3)
    lax.fori_loop(0, outgoing.shape[0], forward, 0, unroll=4)
    mix(1)
    turn(0)
    for copy in result_stores(0):
        copy.start()
    turn(1)
    for copy in result_stores(1):
        copy.start()
    for block in range(total // BLOCK_ROWS):
        device = page_map[0, prior_blocks + block]

        @pl.when(device & (TP - 1) == rank)
        def _():
            slot = device >> TP_BITS
            rows = keyval[pl.ds(block * BLOCK_ROWS, BLOCK_ROWS)]
            trim(slot, fresh - block * BLOCK_ROWS, rows)
            block_store(slot).start()

    for slot in range(outgoing.shape[0]):
        block_store(slot).wait()
    for block in range(total // PROJECT_ROWS):
        for copy in result_stores(block):
            copy.wait()


def project(cache_len, group_len, page_map, hidden_in, norm_gain, w_query, w_keyval, prior):
    rows, model = hidden_in.shape
    half_size = HEAD_SIZE // 2
    frequency = 10000.0 ** (-(np.arange(half_size, dtype=np.float64) * 2.0 / HEAD_SIZE))
    frequency = jnp.asarray(np.tile(frequency, LANES // half_size)[None].astype(np.float32))
    count = page_map.shape[1] // TP
    scalar = pl.BlockSpec(memory_space=pltpu.SMEM)
    vector = pl.BlockSpec(memory_space=pltpu.VMEM)
    far = pl.BlockSpec(memory_space=pltpu.HBM)
    return pl.pallas_call(
        project_kernel,
        out_shape=(
            jax.ShapeDtypeStruct((QUERY_BLOCKS, STACK, HEAD_SIZE), jnp.bfloat16),
            jax.ShapeDtypeStruct((rows, WIDTH), jnp.bfloat16),
            jax.ShapeDtypeStruct((count, BLOCK_ROWS, WIDTH), jnp.bfloat16),
        ),
        in_specs=[scalar, scalar, scalar, far, vector, far, far, vector, far],
        out_specs=[far, far, far],
        scratch_shapes=[
            pltpu.VMEM((QUERY_BLOCKS, STACK, HEAD_SIZE), jnp.bfloat16),
            pltpu.VMEM((rows, WIDTH), jnp.bfloat16),
            pltpu.VMEM((count, BLOCK_ROWS, WIDTH), jnp.bfloat16),
            pltpu.SMEM((count,), jnp.int32),
            pltpu.VMEM((rows, model), jnp.bfloat16),
            pltpu.VMEM((SPAN, model), jnp.bfloat16),
            pltpu.VMEM((model, WIDTH), jnp.bfloat16),
            pltpu.VMEM((rows, model), jnp.bfloat16),
            pltpu.VMEM((rows, 3 * LANES), jnp.float32),
            pltpu.VMEM((rows, WIDTH), jnp.float32),
            pltpu.VMEM((rows, LANES), jnp.float32),
            pltpu.VMEM((rows, LANES), jnp.float32),
            pltpu.SemaphoreType.DMA((rows // NORM_ROWS + 2,)),
            pltpu.SemaphoreType.DMA((count,)),
            pltpu.SemaphoreType.DMA((count,)),
            pltpu.SemaphoreType.DMA((2, rows // PROJECT_ROWS)),
        ],
        compiler_params=pltpu.CompilerParams(vmem_limit_bytes=58 * MIB),
        cost_estimate=pl.CostEstimate(
            flops=2 * rows * model * (SPAN + WIDTH), bytes_accessed=15 * MIB, transcendentals=0
        ),
        name="project",
    )(
        cache_len,
        group_len,
        page_map,
        hidden_in,
        norm_gain,
        w_query.T,
        w_keyval,
        frequency,
        prior,
    )


def attend_kernel(
    cache_len,
    group_len,
    queries_hbm,
    prior,
    fresh_rows,
    heads_out,
    queries,
    raw_keys,
    raw_values,
    keys,
    values,
    top,
    total,
    semaphores,
):
    cached, fresh, rank = cache_len[0], group_len[0], lax.axis_index("tp")
    key_start = pl.multiple_of(key_tile_start(rank) * LANES, LANES)
    value_start = pl.multiple_of(value_tile_start(rank) * LANES, LANES)
    key_shift, value_shift = key_offset(rank), value_offset(rank)
    prior_chunks = (cached + KEY_ROWS - 1) // KEY_ROWS
    blocks = (fresh + QUERY_ROWS - 1) // QUERY_ROWS
    chunk_limit = PRIOR_SLOTS // KEY_ROWS

    def copies(chunk):
        into = pl.ds(chunk * KEY_ROWS, KEY_ROWS)
        return (
            pltpu.make_async_copy(
                prior.at[into, pl.ds(key_start, WINDOW)],
                raw_keys.at[into],
                semaphores.at[0, chunk],
            ),
            pltpu.make_async_copy(
                prior.at[into, pl.ds(value_start, WINDOW)],
                raw_values.at[into],
                semaphores.at[1, chunk],
            ),
        )

    into = pl.ds(PRIOR_SLOTS, NEW_TOKEN_SLOTS)
    fresh_copies = (
        pltpu.make_async_copy(
            fresh_rows.at[:, pl.ds(key_start, WINDOW)],
            raw_keys.at[into],
            semaphores.at[0, chunk_limit],
        ),
        pltpu.make_async_copy(
            fresh_rows.at[:, pl.ds(value_start, WINDOW)],
            raw_values.at[into],
            semaphores.at[1, chunk_limit],
        ),
    )
    fresh_copies += (
        pltpu.make_async_copy(queries_hbm, queries, semaphores.at[0, chunk_limit + 1]),
    )
    for copy in fresh_copies:
        copy.start()
    for chunk in range(chunk_limit):

        @pl.when(chunk < prior_chunks)
        def _():
            for copy in copies(chunk):
                copy.start()

    def prepare(start, live):
        here = pl.ds(start, PREPARE_ROWS)
        lanes = lane_ids(PREPARE_ROWS)
        alive = lax.broadcasted_iota(jnp.int32, (PREPARE_ROWS, LANES), 0) < live
        raw = raw_keys[here].astype(jnp.float32)
        low, high = raw[:, :LANES], raw[:, LANES:]
        spare = raw_keys[0:8].astype(jnp.float32)[0:1]
        low = jnp.where(alive, low, spare[:, :LANES])
        high = jnp.where(alive, high, spare[:, LANES:])
        joined = jnp.where(
            lanes < HEAD_SIZE, pltpu.roll(low, HEAD_SIZE, 1), pltpu.roll(high, HEAD_SIZE, 1)
        )
        pair = jnp.where(key_shift == 0, low, joined)
        keys[:, here] = pair.T.astype(jnp.bfloat16)
        raw = raw_values[here].astype(jnp.float32)
        low, high = raw[:, :LANES], raw[:, LANES:]
        low_turned, high_turned = pltpu.roll(low, HEAD_SIZE, 1), pltpu.roll(high, HEAD_SIZE, 1)
        one = jnp.where(
            value_shift == 0, low, jnp.where(value_shift == HEAD_SIZE, low_turned, high)
        )
        two = jnp.where(
            value_shift == 0, low_turned, jnp.where(value_shift == HEAD_SIZE, high, high_turned)
        )
        for slot, own in enumerate((one, two)):
            own = jnp.where(alive, jnp.where(lanes < HEAD_SIZE, own, 1.0), 0.0)
            values[slot, here] = own.astype(jnp.bfloat16)

    def score(block, head, start, rows):
        which = local_kv(rank, head)
        return jnp.dot(
            queries[block, head * QUERY_ROWS : (head + 1) * QUERY_ROWS],
            keys[pl.ds(pl.multiple_of(which * HEAD_SIZE, HEAD_SIZE), HEAD_SIZE), pl.ds(start, rows)],
            preferred_element_type=jnp.float32,
        )

    def blend(head, start, rows, scores, masked):
        own = slice(head * QUERY_ROWS, (head + 1) * QUERY_ROWS)
        if masked:
            row = lax.broadcasted_iota(jnp.int32, scores.shape, 0)
            column = lax.broadcasted_iota(jnp.int32, scores.shape, 1)
            scores = jnp.where(column <= row, scores, -1e30)
        before = top[own]
        after = jnp.maximum(before, jnp.max(scores, axis=-1, keepdims=True))
        rescale = jnp.exp(before - after)
        chances = jnp.exp(scores - jnp.tile(after, (1, rows // LANES))).astype(jnp.bfloat16)
        top[own] = after
        total[own] = total[own] * rescale + jnp.dot(
            chances,
            values[local_kv(rank, head), pl.ds(start, rows)],
            preferred_element_type=jnp.float32,
        )

    def absorb(block, start, rows, masked):
        pending = score(block, 0, start, rows)
        for head in range(LOCAL):
            following = score(block, head + 1, start, rows) if head + 1 < LOCAL else None
            blend(head, start, rows, pending, masked)
            pending = following

    def query_block(block, carry):
        top[...] = jnp.full_like(top, -1e30)
        total[...] = jnp.zeros_like(total)

        @pl.when(block == 0)
        def _():
            for copy in fresh_copies:
                copy.wait()

            def each(step, inner):
                start = pl.multiple_of(PRIOR_SLOTS + step * PREPARE_ROWS, PREPARE_ROWS)
                prepare(start, PREPARE_ROWS)
                return inner

            lax.fori_loop(0, NEW_TOKEN_SLOTS // PREPARE_ROWS, each, 0)

        def earlier(step, inner):
            start = pl.multiple_of(PRIOR_SLOTS + step * QUERY_ROWS, QUERY_ROWS)
            absorb(block, start, QUERY_ROWS, False)
            return inner

        def cache(step, inner):
            start = pl.multiple_of(step * KEY_ROWS, KEY_ROWS)

            @pl.when(block == 0)
            def _():
                for copy in copies(step):
                    copy.wait()

                def each(part, most):
                    here = pl.multiple_of(start + part * PREPARE_ROWS, PREPARE_ROWS)
                    prepare(here, cached - here)
                    return most

                lax.fori_loop(0, KEY_ROWS // PREPARE_ROWS, each, 0)

            absorb(block, start, KEY_ROWS, False)
            return inner

        start = pl.multiple_of(PRIOR_SLOTS + block * QUERY_ROWS, QUERY_ROWS)
        absorb(block, start, QUERY_ROWS, True)
        lax.fori_loop(0, block, earlier, 0)
        lax.fori_loop(0, prior_chunks, cache, 0)

        lanes = lane_ids(QUERY_ROWS)
        odd = rank % 2 == 1
        plain, turned = [], []
        for head in range(LOCAL):
            sums = total[head * QUERY_ROWS : (head + 1) * QUERY_ROWS]
            swapped = pltpu.roll(sums, HEAD_SIZE, 1)
            plain.append(sums / swapped)
            turned.append(swapped / sums)
        even_pairs = [jnp.where(lanes < HEAD_SIZE, plain[i], turned[i + 1]) for i in (0, 2)]
        odd_pairs = [jnp.where(lanes < HEAD_SIZE, plain[i], turned[i + 1]) for i in (1, 3)]
        single = jnp.where(odd, plain[0], plain[4])
        single_turned = jnp.where(odd, turned[0], turned[4])
        near = (lane_ids(LANES) < HEAD_SIZE) != odd
        for part in range(QUERY_ROWS // PART_ROWS):
            slot = block * (QUERY_ROWS // PART_ROWS) + part
            rows = slice(part * PART_ROWS, (part + 1) * PART_ROWS)
            for tile in range(2):
                pair = jnp.where(odd, odd_pairs[tile][rows], even_pairs[tile][rows])
                heads_out[slot, tile * PART_ROWS : (tile + 1) * PART_ROWS] = pair.astype(
                    jnp.bfloat16
                )
            begin = part * PART_ROWS
            above, below = slice(begin, begin + LANES), slice(begin + LANES, begin + PART_ROWS)
            packed = jnp.where(
                odd,
                jnp.where(near, single_turned[above], single[below]),
                jnp.where(near, single[above], single_turned[below]),
            )
            heads_out[slot, 2 * PART_ROWS :] = packed.astype(jnp.bfloat16)
        return carry

    lax.fori_loop(0, blocks, query_block, 0)

    def idle(slot, carry):
        heads_out[slot] = jnp.zeros((PACKED, LANES), jnp.bfloat16)
        return carry

    parts = QUERY_ROWS // PART_ROWS
    lax.fori_loop(blocks * parts, QUERY_BLOCKS * parts, idle, 0)


def attend(cache_len, group_len, queries, prior, fresh_rows):
    context = PRIOR_SLOTS + NEW_TOKEN_SLOTS
    vector = pl.BlockSpec(memory_space=pltpu.VMEM)
    return pl.pallas_call(
        attend_kernel,
        out_shape=jax.ShapeDtypeStruct(
            (NEW_TOKEN_SLOTS // PART_ROWS, PACKED, LANES), jnp.bfloat16
        ),
        in_specs=[
            pl.BlockSpec(memory_space=pltpu.SMEM),
            pl.BlockSpec(memory_space=pltpu.SMEM),
            pl.BlockSpec(memory_space=pl.ANY),
            pl.BlockSpec(memory_space=pltpu.HBM),
            pl.BlockSpec(memory_space=pl.ANY),
        ],
        out_specs=vector,
        scratch_shapes=[
            pltpu.VMEM(queries.shape, queries.dtype),
            pltpu.VMEM((context, WINDOW), jnp.bfloat16),
            pltpu.VMEM((context, WINDOW), jnp.bfloat16),
            pltpu.VMEM((LANES, context), jnp.bfloat16),
            pltpu.VMEM((2, context, LANES), jnp.bfloat16),
            pltpu.VMEM((STACK, LANES), jnp.float32),
            pltpu.VMEM((STACK, LANES), jnp.float32),
            pltpu.SemaphoreType.DMA((2, PRIOR_SLOTS // KEY_ROWS + 2)),
        ],
        compiler_params=pltpu.CompilerParams(vmem_limit_bytes=56 * MIB),
        cost_estimate=pl.CostEstimate(
            flops=4 * 5120 * 7680 * 256, bytes_accessed=12 * MIB, transcendentals=5120 * 7680
        ),
        name="attend",
    )(cache_len, group_len, queries, prior, fresh_rows)


def store_kernel(received, w_out, hidden, decode, w_near, hidden_near, semaphores):
    rows = hidden_near.shape[0]
    begin = pl.multiple_of(lax.axis_index("tp") * rows, rows)
    copies = (
        pltpu.make_async_copy(w_out, w_near, semaphores.at[0]),
        pltpu.make_async_copy(received, decode, semaphores.at[1]),
        pltpu.make_async_copy(hidden.at[pl.ds(begin, rows)], hidden_near, semaphores.at[2]),
    )
    for copy in copies:
        copy.start()
    for copy in copies:
        copy.wait()


def store_blocks(received, w_out, hidden_in):
    vector = pl.BlockSpec(memory_space=pltpu.VMEM)
    far = pl.BlockSpec(memory_space=pltpu.HBM)
    return pl.pallas_call(
        store_kernel,
        out_shape=(
            jax.ShapeDtypeStruct(received.shape, received.dtype),
            jax.ShapeDtypeStruct(w_out.shape, w_out.dtype),
            jax.ShapeDtypeStruct((PART_ROWS, hidden_in.shape[1]), hidden_in.dtype),
        ),
        in_specs=[vector, far, far],
        out_specs=[far, vector, vector],
        scratch_shapes=[pltpu.SemaphoreType.DMA((3,))],
        compiler_params=pltpu.CompilerParams(vmem_limit_bytes=STORE_LIMIT * MIB),
        cost_estimate=pl.CostEstimate(flops=0, bytes_accessed=12 * MIB, transcendentals=0),
        name="store_blocks",
    )(received, w_out, hidden_in)


def finish_kernel(group_len, own, *rest):
    travelled = rest[: TP - 1]
    w_out, hidden, result, heads, joined = rest[TP - 1 :]
    rank, fresh = lax.axis_index("tp"), group_len[0]
    rows = result.shape[0]
    wide = FINISH_COLUMNS
    steps = result.shape[1] // wide
    for shift, source in enumerate((own,) + tuple(travelled)):
        heads[(rank + TP - shift) & (TP - 1)] = source[...]
    low = lane_ids(LANES) < HEAD_SIZE
    for pair in range(2):
        first, second = heads.at[2 * pair], heads.at[2 * pair + 1]
        for tile in range(2):
            source = slice(tile * PART_ROWS, (tile + 1) * PART_ROWS)
            columns = (5 * pair + tile) * LANES
            joined[:, columns : columns + LANES] = first[source]
            joined[:, columns + 3 * LANES : columns + 4 * LANES] = second[source]
        one = first[2 * PART_ROWS :].astype(jnp.float32)
        two = second[2 * PART_ROWS :].astype(jnp.float32)
        columns = (5 * pair + 2) * LANES
        joined[:LANES, columns : columns + LANES] = jnp.where(low, one, two).astype(jnp.bfloat16)
        one, two = pltpu.roll(one, HEAD_SIZE, 1), pltpu.roll(two, HEAD_SIZE, 1)
        joined[LANES:, columns : columns + LANES] = jnp.where(low, one, two).astype(jnp.bfloat16)
    alive = lax.broadcasted_iota(jnp.int32, (rows, wide), 0) + rank * rows < fresh
    for step in range(steps):
        columns = slice(step * wide, (step + 1) * wide)
        mixed = jnp.dot(joined[...], w_out[:, columns], preferred_element_type=jnp.float32)
        value = hidden[:, columns].astype(jnp.float32) + mixed
        result[:, columns] = jnp.where(alive, value, 0.0).astype(jnp.bfloat16)


def finish(group_len, heads, w_out, hidden):
    model = w_out.shape[1]
    vector = pl.BlockSpec(memory_space=pltpu.VMEM)
    return pl.pallas_call(
        finish_kernel,
        out_shape=jax.ShapeDtypeStruct((PART_ROWS, model), jnp.bfloat16),
        in_specs=[pl.BlockSpec(memory_space=pltpu.SMEM)] + [vector] * (TP + 2),
        out_specs=vector,
        scratch_shapes=[
            pltpu.VMEM((TP, PACKED, LANES), jnp.bfloat16),
            pltpu.VMEM((PART_ROWS, w_out.shape[0]), jnp.bfloat16),
        ],
        compiler_params=pltpu.CompilerParams(vmem_limit_bytes=FINISH_LIMIT * MIB),
        cost_estimate=pl.CostEstimate(
            flops=2 * PART_ROWS * w_out.shape[0] * model,
            bytes_accessed=8 * MIB,
            transcendentals=0,
        ),
        name="finish",
    )(group_len, *heads, w_out, hidden)


def shards(
    hidden_in,
    norm_gain,
    w_query,
    key_value_weight,
    w_out,
    prior_cache,
    cache_len,
    group_len,
    page_map,
):
    prior = prior_cache[0]
    queries, keyval, outgoing = project(
        cache_len, group_len, page_map, hidden_in, norm_gain, w_query, key_value_weight, prior
    )
    outgoing, queries = lax.optimization_barrier((outgoing, queries))
    received = lax.all_to_all(outgoing, "req", split_axis=0, concat_axis=0, tiled=True)
    attended = attend(cache_len, group_len, queries, prior, keyval)
    attended, received = lax.optimization_barrier((attended, received))
    rank = lax.axis_index("tp")
    heads = [lax.dynamic_index_in_dim(attended, rank, 0, keepdims=False)]
    for shift in range(1, TP):
        part = lax.dynamic_index_in_dim(attended, (rank + shift) % TP, 0, keepdims=False)
        pairs = [(source, (source + shift) % TP) for source in range(TP)]
        heads.append(lax.ppermute(part, "tp", pairs))
    decode_kv, w_near, hidden_near = store_blocks(received, w_out, hidden_in)
    hidden_out = finish(group_len, heads, w_near, hidden_near)
    return (hidden_out, decode_kv[None])


def solution(mesh):
    placed = (
        P("req", None),
        P(),
        P(None, "tp"),
        P(),
        P(),
        P("req", None, None),
        P("req"),
        P("req"),
        P("req", None),
    )
    return jax.shard_map(
        shards,
        mesh=mesh,
        in_specs=placed,
        out_specs=(P(("req", "tp"), None), P(("req", "tp"), None, None, None)),
        check_vma=False,
    )
```

```python
import jax
import jax.numpy as jnp
import numpy as np
from jax import lax
from jax.experimental import pallas as pl
from jax.experimental.pallas import tpu as pltpu
from jax.sharding import PartitionSpec as P

QUERY_HEAD_COUNT = 20
KEY_VALUE_HEADS = 5
HEAD_SIZE = 64
GROUP = QUERY_HEAD_COUNT // KEY_VALUE_HEADS
NEW_TOKEN_SLOTS = 1024
PRIOR_SLOTS = 7168
SPAN = KEY_VALUE_HEADS * HEAD_SIZE
WIDTH = 2 * SPAN
LANES = 128
WINDOW = 256
LOCAL = 5
TP = QUERY_HEAD_COUNT // LOCAL
TP_BITS = TP.bit_length() - 1
KEPT = 1 << 20
QUERY_ROWS = 512
QUERY_BLOCKS = NEW_TOKEN_SLOTS // QUERY_ROWS
KEY_ROWS = 1792
PREPARE_ROWS = 256
PROJECT_ROWS = 512
NORM_ROWS = 256
PART_ROWS = 256
FINISH_COLUMNS = 512
FINISH_LIMIT = 24
STORE_LIMIT = 24
PACKED = PART_ROWS * LOCAL // 2
BLOCK_ROWS = 64
MIB = 1 << 20


def lane_ids(rows):
    return lax.broadcasted_iota(jnp.int32, (rows, LANES), 1)


def local_kv(rank, head):
    return (rank * LOCAL + head) // GROUP - rank


def key_tile_start(rank):
    return rank // 2


def value_tile_start(rank):
    return jnp.where(rank == 0, 2, 3)


def key_offset(rank):
    return rank * HEAD_SIZE - key_tile_start(rank) * LANES


def value_offset(rank):
    return SPAN + rank * HEAD_SIZE - value_tile_start(rank) * LANES


def rotate(tile, cosine, sine):
    low = lane_ids(tile.shape[0]) % HEAD_SIZE < HEAD_SIZE // 2
    half = HEAD_SIZE // 2
    other = jnp.where(low, pltpu.roll(tile, LANES - half, 1), pltpu.roll(tile, half, 1))
    return tile * cosine + other * sine


def project_kernel(
    cache_len,
    group_len,
    page_map,
    hidden_hbm,
    gain,
    w_query_hbm,
    w_keyval_hbm,
    frequency,
    prior,
    queries_hbm,
    keyval_hbm,
    outgoing_hbm,
    own_hidden,
    queries,
    keyval,
    outgoing,
    live_rows,
    hidden,
    w_query,
    w_keyval,
    normed,
    mixed_q,
    mixed_kv,
    cosine,
    sine,
    semaphores,
    block_semaphores,
    store_semaphores,
    result_semaphores,
):
    cached, fresh = cache_len[0], group_len[0]
    rank = lax.axis_index("tp")
    total = hidden.shape[0]
    pieces = total // NORM_ROWS
    loads = [
        pltpu.make_async_copy(
            hidden_hbm.at[pl.ds(piece * NORM_ROWS, NORM_ROWS)],
            hidden.at[pl.ds(piece * NORM_ROWS, NORM_ROWS)],
            semaphores.at[piece],
        )
        for piece in range(pieces)
    ]
    weights = [
        pltpu.make_async_copy(w_keyval_hbm, w_keyval, semaphores.at[pieces]),
        pltpu.make_async_copy(w_query_hbm, w_query, semaphores.at[pieces + 1]),
    ]
    for copy in loads[:2] + weights + loads[2:]:
        copy.start()

    def prior_copy(block, slot):
        start = pl.multiple_of(block * BLOCK_ROWS, BLOCK_ROWS)
        return pltpu.make_async_copy(
            prior.at[pl.ds(start, BLOCK_ROWS)], outgoing.at[slot], block_semaphores.at[slot]
        )

    def block_store(slot):
        return pltpu.make_async_copy(
            outgoing.at[slot], outgoing_hbm.at[slot], store_semaphores.at[slot]
        )

    def send(block, carry):
        device = page_map[0, block]

        @pl.when(device & (TP - 1) == rank)
        def _():
            slot = device >> TP_BITS
            live = cached - block * BLOCK_ROWS
            live_rows[slot] = live

            @pl.when(live > 0)
            def _():
                prior_copy(block, slot).start()

        return carry

    prior_blocks = PRIOR_SLOTS // BLOCK_ROWS
    lax.fori_loop(0, prior_blocks, send, 0, unroll=8)
    for block in range(total // BLOCK_ROWS):
        device = page_map[0, prior_blocks + block]

        @pl.when(device & (TP - 1) == rank)
        def _():
            live_rows[device >> TP_BITS] = KEPT

    count = 32
    steps = lax.broadcasted_iota(jnp.int32, (count, LANES), 0)
    coarse = (steps * count + cached).astype(jnp.float32) * frequency[...]
    fine = steps.astype(jnp.float32) * frequency[...]
    coarse_cos, coarse_sin = jnp.cos(coarse), jnp.sin(coarse)
    fine_cos, fine_sin = jnp.cos(fine), jnp.sin(fine)
    low_half = lane_ids(count) % HEAD_SIZE < HEAD_SIZE // 2
    for step in range(total // count):
        here = pl.ds(step * count, count)
        far_cos, far_sin = coarse_cos[step : step + 1], coarse_sin[step : step + 1]
        cosine[here] = far_cos * fine_cos - far_sin * fine_sin
        both = far_sin * fine_cos + far_cos * fine_sin
        sine[here] = jnp.where(low_half, -both, both)

    def norm(piece):
        here = pl.ds(piece * NORM_ROWS, NORM_ROWS)
        value = hidden[here].astype(jnp.float32)
        scale = lax.rsqrt(jnp.mean(value * value, axis=-1, keepdims=True) + 1e-05)
        normed[here] = (value * scale * scale_row).astype(jnp.bfloat16)

    scale_row = gain[...].astype(jnp.float32).reshape(1, -1)
    lanes = lane_ids(PROJECT_ROWS)

    def mix(block):
        here = pl.ds(block * PROJECT_ROWS, PROJECT_ROWS)
        rows = normed[here]
        mixed_kv[here] = jnp.dot(rows, w_keyval[...], preferred_element_type=jnp.float32)
        mixed_q[here, :SPAN] = lax.dot_general(
            rows, w_query[...], (((1,), (1,)), ((), ())), preferred_element_type=jnp.float32
        )

    def turn(block):
        here = pl.ds(block * PROJECT_ROWS, PROJECT_ROWS)
        cos, sin = cosine[here], sine[here]
        for tile in range(WIDTH // LANES):
            columns = slice(tile * LANES, (tile + 1) * LANES)
            raw = mixed_kv[here, columns]
            if tile < 2:
                raw = rotate(raw, cos, sin)
            elif tile == 2:
                raw = jnp.where(lanes < HEAD_SIZE, rotate(raw, cos, sin), raw)
            keyval[here, columns] = raw.astype(jnp.bfloat16)
        for tile in range(3):
            raw = mixed_q[here, tile * LANES : (tile + 1) * LANES]
            turned = rotate(raw, cos, sin) * HEAD_SIZE**-0.5
            for head in range(2 * tile, min(2 * tile + 2, LOCAL)):
                own = turned if head % 2 == 0 else pltpu.roll(turned, HEAD_SIZE, 1)
                queries[head, here] = own[:, :HEAD_SIZE].astype(jnp.bfloat16)

    def trim(slot, live, value):
        rows = lax.broadcasted_iota(jnp.int32, (BLOCK_ROWS, WIDTH), 0)
        outgoing[slot] = jnp.where(rows < live, value.astype(jnp.float32), 0.0).astype(jnp.bfloat16)

    def forward(slot, carry):
        live = live_rows[slot]

        @pl.when((live > 0) & (live < KEPT))
        def _():
            prior_copy(0, slot).wait()

        @pl.when((live > 0) & (live < BLOCK_ROWS))
        def _():
            trim(slot, live, outgoing[slot])

        @pl.when(live <= 0)
        def _():
            outgoing[slot] = jnp.zeros((BLOCK_ROWS, WIDTH), jnp.bfloat16)

        @pl.when(live < KEPT)
        def _():
            block_store(slot).start()

        return carry

    def result_stores(block):
        here = pl.ds(block * PROJECT_ROWS, PROJECT_ROWS)
        return [
            pltpu.make_async_copy(
                keyval.at[here], keyval_hbm.at[here], result_semaphores.at[0, block]
            ),
            pltpu.make_async_copy(
                queries.at[:, here], queries_hbm.at[:, here], result_semaphores.at[1, block]
            ),
        ]

    for piece in range(2):
        loads[piece].wait()
        norm(piece)
    for copy in weights + loads[2:]:
        copy.wait()
    rows = own_hidden.shape[0]
    own_store = pltpu.make_async_copy(
        hidden.at[pl.ds(pl.multiple_of(rank * rows, rows), rows)],
        own_hidden,
        semaphores.at[pieces + 2],
    )
    own_store.start()
    mix(0)
    norm(2)
    norm(3)
    lax.fori_loop(0, outgoing.shape[0], forward, 0, unroll=4)
    mix(1)
    turn(0)
    for copy in result_stores(0):
        copy.start()
    turn(1)
    for copy in result_stores(1):
        copy.start()
    for block in range(total // BLOCK_ROWS):
        device = page_map[0, prior_blocks + block]

        @pl.when(device & (TP - 1) == rank)
        def _():
            slot = device >> TP_BITS
            rows = keyval[pl.ds(block * BLOCK_ROWS, BLOCK_ROWS)]
            trim(slot, fresh - block * BLOCK_ROWS, rows)
            block_store(slot).start()

    own_store.wait()
    for slot in range(outgoing.shape[0]):
        block_store(slot).wait()
    for block in range(total // PROJECT_ROWS):
        for copy in result_stores(block):
            copy.wait()


def project(cache_len, group_len, page_map, hidden_in, norm_gain, w_query, w_keyval, prior):
    rows, model = hidden_in.shape
    half_size = HEAD_SIZE // 2
    frequency = 10000.0 ** (-(np.arange(half_size, dtype=np.float64) * 2.0 / HEAD_SIZE))
    frequency = jnp.asarray(np.tile(frequency, LANES // half_size)[None].astype(np.float32))
    count = page_map.shape[1] // TP
    scalar = pl.BlockSpec(memory_space=pltpu.SMEM)
    vector = pl.BlockSpec(memory_space=pltpu.VMEM)
    far = pl.BlockSpec(memory_space=pltpu.HBM)
    return pl.pallas_call(
        project_kernel,
        out_shape=(
            jax.ShapeDtypeStruct((LOCAL, rows, HEAD_SIZE), jnp.bfloat16),
            jax.ShapeDtypeStruct((rows, WIDTH), jnp.bfloat16),
            jax.ShapeDtypeStruct((count, BLOCK_ROWS, WIDTH), jnp.bfloat16),
            jax.ShapeDtypeStruct((rows // TP, model), jnp.bfloat16),
        ),
        in_specs=[scalar, scalar, scalar, far, vector, far, far, vector, far],
        out_specs=[far, far, far, far],
        scratch_shapes=[
            pltpu.VMEM((LOCAL, rows, HEAD_SIZE), jnp.bfloat16),
            pltpu.VMEM((rows, WIDTH), jnp.bfloat16),
            pltpu.VMEM((count, BLOCK_ROWS, WIDTH), jnp.bfloat16),
            pltpu.SMEM((count,), jnp.int32),
            pltpu.VMEM((rows, model), jnp.bfloat16),
            pltpu.VMEM((SPAN, model), jnp.bfloat16),
            pltpu.VMEM((model, WIDTH), jnp.bfloat16),
            pltpu.VMEM((rows, model), jnp.bfloat16),
            pltpu.VMEM((rows, 3 * LANES), jnp.float32),
            pltpu.VMEM((rows, WIDTH), jnp.float32),
            pltpu.VMEM((rows, LANES), jnp.float32),
            pltpu.VMEM((rows, LANES), jnp.float32),
            pltpu.SemaphoreType.DMA((rows // NORM_ROWS + 3,)),
            pltpu.SemaphoreType.DMA((count,)),
            pltpu.SemaphoreType.DMA((count,)),
            pltpu.SemaphoreType.DMA((2, rows // PROJECT_ROWS)),
        ],
        compiler_params=pltpu.CompilerParams(vmem_limit_bytes=58 * MIB),
        cost_estimate=pl.CostEstimate(
            flops=2 * rows * model * (SPAN + WIDTH), bytes_accessed=15 * MIB, transcendentals=0
        ),
        name="project",
    )(
        cache_len,
        group_len,
        page_map,
        hidden_in,
        norm_gain,
        w_query.T,
        w_keyval,
        frequency,
        prior,
    )


def attend_kernel(
    cache_len,
    group_len,
    queries_hbm,
    prior,
    fresh_rows,
    *rest,
):
    outs = rest[:TP]
    heads_out, queries, raw_keys, raw_values, keys, values, top, total, semaphores = rest[TP:]
    cached, fresh, rank = cache_len[0], group_len[0], lax.axis_index("tp")
    key_start = pl.multiple_of(key_tile_start(rank) * LANES, LANES)
    value_start = pl.multiple_of(value_tile_start(rank) * LANES, LANES)
    key_shift, value_shift = key_offset(rank), value_offset(rank)
    prior_chunks = (cached + KEY_ROWS - 1) // KEY_ROWS
    blocks = (fresh + QUERY_ROWS - 1) // QUERY_ROWS
    chunk_limit = PRIOR_SLOTS // KEY_ROWS

    def copies(chunk):
        into = pl.ds(chunk * KEY_ROWS, KEY_ROWS)
        return (
            pltpu.make_async_copy(
                prior.at[into, pl.ds(key_start, WINDOW)],
                raw_keys.at[into],
                semaphores.at[0, chunk],
            ),
            pltpu.make_async_copy(
                prior.at[into, pl.ds(value_start, WINDOW)],
                raw_values.at[into],
                semaphores.at[1, chunk],
            ),
        )

    into = pl.ds(PRIOR_SLOTS, NEW_TOKEN_SLOTS)
    fresh_copies = (
        pltpu.make_async_copy(
            fresh_rows.at[:, pl.ds(key_start, WINDOW)],
            raw_keys.at[into],
            semaphores.at[0, chunk_limit],
        ),
        pltpu.make_async_copy(
            fresh_rows.at[:, pl.ds(value_start, WINDOW)],
            raw_values.at[into],
            semaphores.at[1, chunk_limit],
        ),
    )
    fresh_copies += (
        pltpu.make_async_copy(queries_hbm, queries, semaphores.at[0, chunk_limit + 1]),
    )
    for copy in fresh_copies:
        copy.start()
    for chunk in range(chunk_limit):

        @pl.when(chunk < prior_chunks)
        def _():
            for copy in copies(chunk):
                copy.start()

    def prepare(start, live):
        here = pl.ds(start, PREPARE_ROWS)
        lanes = lane_ids(PREPARE_ROWS)
        alive = lax.broadcasted_iota(jnp.int32, (PREPARE_ROWS, LANES), 0) < live
        raw = raw_keys[here].astype(jnp.float32)
        low, high = raw[:, :LANES], raw[:, LANES:]
        spare = raw_keys[0:8].astype(jnp.float32)[0:1]
        low = jnp.where(alive, low, spare[:, :LANES])
        high = jnp.where(alive, high, spare[:, LANES:])
        joined = jnp.where(
            lanes < HEAD_SIZE, pltpu.roll(low, HEAD_SIZE, 1), pltpu.roll(high, HEAD_SIZE, 1)
        )
        pair = jnp.where(key_shift == 0, low, joined)
        keys[:, here] = pair.T.astype(jnp.bfloat16)
        raw = raw_values[here].astype(jnp.float32)
        low, high = raw[:, :LANES], raw[:, LANES:]
        low_turned, high_turned = pltpu.roll(low, HEAD_SIZE, 1), pltpu.roll(high, HEAD_SIZE, 1)
        one = jnp.where(
            value_shift == 0, low, jnp.where(value_shift == HEAD_SIZE, low_turned, high)
        )
        two = jnp.where(
            value_shift == 0, low_turned, jnp.where(value_shift == HEAD_SIZE, high, high_turned)
        )
        for slot, own in enumerate((one, two)):
            own = jnp.where(alive, jnp.where(lanes < HEAD_SIZE, own, 1.0), 0.0)
            values[slot, here] = own.astype(jnp.bfloat16)

    def score(span, head, start, rows):
        which = local_kv(rank, head)
        return jnp.dot(
            queries[head, span],
            keys[pl.ds(pl.multiple_of(which * HEAD_SIZE, HEAD_SIZE), HEAD_SIZE), pl.ds(start, rows)],
            preferred_element_type=jnp.float32,
        )

    def blend(span, head, start, rows, scores, masked):
        if masked:
            row = lax.broadcasted_iota(jnp.int32, scores.shape, 0)
            column = lax.broadcasted_iota(jnp.int32, scores.shape, 1)
            scores = jnp.where(column <= row, scores, -1e30)
        before = top[head, span]
        after = jnp.maximum(before, jnp.max(scores, axis=-1, keepdims=True))
        rescale = jnp.exp(before - after)
        chances = jnp.exp(scores - jnp.tile(after, (1, rows // LANES))).astype(jnp.bfloat16)
        top[head, span] = after
        total[head, span] = total[head, span] * rescale + jnp.dot(
            chances,
            values[local_kv(rank, head), pl.ds(start, rows)],
            preferred_element_type=jnp.float32,
        )

    def absorb(span, start, rows, masked=False):
        pieces = [
            (head, slice(begin, begin + QUERY_ROWS))
            for head in range(LOCAL)
            for begin in range(span.start, span.stop, QUERY_ROWS)
        ]
        pending = score(pieces[0][1], pieces[0][0], start, rows)
        for index, (head, piece) in enumerate(pieces):
            following = None
            if index + 1 < len(pieces):
                following = score(pieces[index + 1][1], pieces[index + 1][0], start, rows)
            blend(piece, head, start, rows, pending, masked)
            pending = following

    lower, upper = slice(0, QUERY_ROWS), slice(QUERY_ROWS, 2 * QUERY_ROWS)
    everything = slice(0, 2 * QUERY_ROWS)
    top[...] = jnp.full_like(top, -1e30)
    total[...] = jnp.zeros_like(total)
    for copy in fresh_copies:
        copy.wait()

    def prepare_fresh(step, inner):
        start = pl.multiple_of(PRIOR_SLOTS + step * PREPARE_ROWS, PREPARE_ROWS)
        prepare(start, PREPARE_ROWS)
        return inner

    lax.fori_loop(0, NEW_TOKEN_SLOTS // PREPARE_ROWS, prepare_fresh, 0)
    absorb(lower, PRIOR_SLOTS, QUERY_ROWS, True)

    @pl.when(blocks > 1)
    def _():
        absorb(upper, PRIOR_SLOTS, QUERY_ROWS)
        absorb(upper, PRIOR_SLOTS + QUERY_ROWS, QUERY_ROWS, True)

    def cache(step, carry):
        start = pl.multiple_of(step * KEY_ROWS, KEY_ROWS)
        for copy in copies(step):
            copy.wait()

        def each(part, most):
            here = pl.multiple_of(start + part * PREPARE_ROWS, PREPARE_ROWS)
            prepare(here, cached - here)
            return most

        lax.fori_loop(0, KEY_ROWS // PREPARE_ROWS, each, 0)

        @pl.when(blocks > 1)
        def _():
            absorb(everything, start, KEY_ROWS)

        @pl.when(blocks <= 1)
        def _():
            absorb(lower, start, KEY_ROWS)

        return carry

    lax.fori_loop(0, prior_chunks, cache, 0)

    def query_block(block, carry):
        here = pl.ds(pl.multiple_of(block * QUERY_ROWS, QUERY_ROWS), QUERY_ROWS)
        lanes = lane_ids(QUERY_ROWS)
        odd = rank % 2 == 1
        plain, turned = [], []
        for head in range(LOCAL):
            sums = total[head, here]
            swapped = pltpu.roll(sums, HEAD_SIZE, 1)
            plain.append(sums / swapped)
            turned.append(swapped / sums)
        even_pairs = [jnp.where(lanes < HEAD_SIZE, plain[i], turned[i + 1]) for i in (0, 2)]
        odd_pairs = [jnp.where(lanes < HEAD_SIZE, plain[i], turned[i + 1]) for i in (1, 3)]
        single = jnp.where(odd, plain[0], plain[4])
        single_turned = jnp.where(odd, turned[0], turned[4])
        near = (lane_ids(LANES) < HEAD_SIZE) != odd
        for part in range(QUERY_ROWS // PART_ROWS):
            slot = (block * (QUERY_ROWS // PART_ROWS) + part + TP - rank) & (TP - 1)
            rows = slice(part * PART_ROWS, (part + 1) * PART_ROWS)
            for tile in range(2):
                pair = jnp.where(odd, odd_pairs[tile][rows], even_pairs[tile][rows])
                heads_out[slot, tile * PART_ROWS : (tile + 1) * PART_ROWS] = pair.astype(
                    jnp.bfloat16
                )
            begin = part * PART_ROWS
            above, below = slice(begin, begin + LANES), slice(begin + LANES, begin + PART_ROWS)
            packed = jnp.where(
                odd,
                jnp.where(near, single_turned[above], single[below]),
                jnp.where(near, single[above], single_turned[below]),
            )
            heads_out[slot, 2 * PART_ROWS :] = packed.astype(jnp.bfloat16)
        return carry

    lax.fori_loop(0, blocks, query_block, 0)

    def idle(part, carry):
        heads_out[(part + TP - rank) & (TP - 1)] = jnp.zeros((PACKED, LANES), jnp.bfloat16)
        return carry

    parts = QUERY_ROWS // PART_ROWS
    lax.fori_loop(blocks * parts, QUERY_BLOCKS * parts, idle, 0)
    for shift, out in enumerate(outs):
        out[...] = heads_out[shift]


def attend(cache_len, group_len, queries, prior, fresh_rows):
    context = PRIOR_SLOTS + NEW_TOKEN_SLOTS
    vector = pl.BlockSpec(memory_space=pltpu.VMEM)
    return pl.pallas_call(
        attend_kernel,
        out_shape=[jax.ShapeDtypeStruct((PACKED, LANES), jnp.bfloat16)] * TP,
        in_specs=[
            pl.BlockSpec(memory_space=pltpu.SMEM),
            pl.BlockSpec(memory_space=pltpu.SMEM),
            pl.BlockSpec(memory_space=pl.ANY),
            pl.BlockSpec(memory_space=pltpu.HBM),
            pl.BlockSpec(memory_space=pl.ANY),
        ],
        out_specs=[vector] * TP,
        scratch_shapes=[
            pltpu.VMEM((TP, PACKED, LANES), jnp.bfloat16),
            pltpu.VMEM(queries.shape, queries.dtype),
            pltpu.VMEM((context, WINDOW), jnp.bfloat16),
            pltpu.VMEM((context, WINDOW), jnp.bfloat16),
            pltpu.VMEM((LANES, context), jnp.bfloat16),
            pltpu.VMEM((2, context, LANES), jnp.bfloat16),
            pltpu.VMEM((LOCAL, NEW_TOKEN_SLOTS, LANES), jnp.float32),
            pltpu.VMEM((LOCAL, NEW_TOKEN_SLOTS, LANES), jnp.float32),
            pltpu.SemaphoreType.DMA((2, PRIOR_SLOTS // KEY_ROWS + 2)),
        ],
        compiler_params=pltpu.CompilerParams(vmem_limit_bytes=56 * MIB),
        cost_estimate=pl.CostEstimate(
            flops=4 * 5120 * 7680 * 256, bytes_accessed=12 * MIB, transcendentals=5120 * 7680
        ),
        name="attend",
    )(cache_len, group_len, queries, prior, fresh_rows)


def store_kernel(received, w_out, decode, w_near, semaphores):
    copies = (
        pltpu.make_async_copy(w_out, w_near, semaphores.at[0]),
        pltpu.make_async_copy(received, decode, semaphores.at[1]),
    )
    for copy in copies:
        copy.start()
    for copy in copies:
        copy.wait()


def store_blocks(received, w_out):
    vector = pl.BlockSpec(memory_space=pltpu.VMEM)
    far = pl.BlockSpec(memory_space=pltpu.HBM)
    return pl.pallas_call(
        store_kernel,
        out_shape=(
            jax.ShapeDtypeStruct(received.shape, received.dtype),
            jax.ShapeDtypeStruct(w_out.shape, w_out.dtype),
        ),
        in_specs=[vector, far],
        out_specs=[far, vector],
        scratch_shapes=[pltpu.SemaphoreType.DMA((2,))],
        compiler_params=pltpu.CompilerParams(vmem_limit_bytes=STORE_LIMIT * MIB),
        cost_estimate=pl.CostEstimate(flops=0, bytes_accessed=12 * MIB, transcendentals=0),
        name="store_blocks",
    )(received, w_out)


def finish_kernel(group_len, own, *rest):
    travelled = rest[: TP - 1]
    w_out, hidden, result, heads, joined = rest[TP - 1 :]
    rank, fresh = lax.axis_index("tp"), group_len[0]
    rows = result.shape[0]
    wide = FINISH_COLUMNS
    steps = result.shape[1] // wide
    for shift, source in enumerate((own,) + tuple(travelled)):
        heads[(rank + TP - shift) & (TP - 1)] = source[...]
    low = lane_ids(LANES) < HEAD_SIZE
    for pair in range(2):
        first, second = heads.at[2 * pair], heads.at[2 * pair + 1]
        for tile in range(2):
            source = slice(tile * PART_ROWS, (tile + 1) * PART_ROWS)
            columns = (5 * pair + tile) * LANES
            joined[:, columns : columns + LANES] = first[source]
            joined[:, columns + 3 * LANES : columns + 4 * LANES] = second[source]
        one = first[2 * PART_ROWS :].astype(jnp.float32)
        two = second[2 * PART_ROWS :].astype(jnp.float32)
        columns = (5 * pair + 2) * LANES
        joined[:LANES, columns : columns + LANES] = jnp.where(low, one, two).astype(jnp.bfloat16)
        one, two = pltpu.roll(one, HEAD_SIZE, 1), pltpu.roll(two, HEAD_SIZE, 1)
        joined[LANES:, columns : columns + LANES] = jnp.where(low, one, two).astype(jnp.bfloat16)
    alive = lax.broadcasted_iota(jnp.int32, (rows, wide), 0) + rank * rows < fresh
    for step in range(steps):
        columns = slice(step * wide, (step + 1) * wide)
        mixed = jnp.dot(joined[...], w_out[:, columns], preferred_element_type=jnp.float32)
        value = hidden[:, columns].astype(jnp.float32) + mixed
        result[:, columns] = jnp.where(alive, value, 0.0).astype(jnp.bfloat16)


def finish(group_len, heads, w_out, hidden):
    model = w_out.shape[1]
    vector = pl.BlockSpec(memory_space=pltpu.VMEM)
    return pl.pallas_call(
        finish_kernel,
        out_shape=jax.ShapeDtypeStruct((PART_ROWS, model), jnp.bfloat16),
        in_specs=[pl.BlockSpec(memory_space=pltpu.SMEM)] + [vector] * (TP + 2),
        out_specs=vector,
        scratch_shapes=[
            pltpu.VMEM((TP, PACKED, LANES), jnp.bfloat16),
            pltpu.VMEM((PART_ROWS, w_out.shape[0]), jnp.bfloat16),
        ],
        compiler_params=pltpu.CompilerParams(vmem_limit_bytes=FINISH_LIMIT * MIB),
        cost_estimate=pl.CostEstimate(
            flops=2 * PART_ROWS * w_out.shape[0] * model,
            bytes_accessed=8 * MIB,
            transcendentals=0,
        ),
        name="finish",
    )(group_len, *heads, w_out, hidden)


def shards(
    hidden_in,
    norm_gain,
    w_query,
    key_value_weight,
    w_out,
    prior_cache,
    cache_len,
    group_len,
    page_map,
):
    prior = prior_cache[0]
    queries, keyval, outgoing, own_hidden = project(
        cache_len, group_len, page_map, hidden_in, norm_gain, w_query, key_value_weight, prior
    )
    outgoing, queries = lax.optimization_barrier((outgoing, queries))
    received = lax.all_to_all(outgoing, "req", split_axis=0, concat_axis=0, tiled=True)
    attended = attend(cache_len, group_len, queries, prior, keyval)
    attended, received = lax.optimization_barrier((attended, received))
    heads = [attended[0]]
    for shift in range(1, TP):
        pairs = [(source, (source + shift) % TP) for source in range(TP)]
        heads.append(lax.ppermute(attended[shift], "tp", pairs))
    decode_kv, w_near = store_blocks(received, w_out)
    hidden_out = finish(group_len, heads, w_near, own_hidden)
    return (hidden_out, decode_kv[None])


def solution(mesh):
    placed = (
        P("req", None),
        P(),
        P(None, "tp"),
        P(),
        P(),
        P("req", None, None),
        P("req"),
        P("req"),
        P("req", None),
    )
    return jax.shard_map(
        shards,
        mesh=mesh,
        in_specs=placed,
        out_specs=(P(("req", "tp"), None), P(("req", "tp"), None, None, None)),
        check_vma=False,
    )
```

```python
import jax
import jax.numpy as jnp
import numpy as np
from jax import lax
from jax.experimental import pallas as pl
from jax.experimental.pallas import tpu as pltpu
from jax.sharding import PartitionSpec as P

QUERY_HEAD_COUNT = 20
KEY_VALUE_HEADS = 5
HEAD_SIZE = 64
SCORE_SCALE = float(HEAD_SIZE**-0.5 * np.log2(np.e))
GROUP = QUERY_HEAD_COUNT // KEY_VALUE_HEADS
NEW_TOKEN_SLOTS = 1024
PRIOR_SLOTS = 7168
SPAN = KEY_VALUE_HEADS * HEAD_SIZE
WIDTH = 2 * SPAN
LANES = 128
WINDOW = 256
LOCAL = 5
TP = QUERY_HEAD_COUNT // LOCAL
TP_BITS = TP.bit_length() - 1
KEPT = 1 << 20
QUERY_ROWS = 512
QUERY_BLOCKS = NEW_TOKEN_SLOTS // QUERY_ROWS
KEY_ROWS = 1792
PREPARE_ROWS = 256
PROJECT_ROWS = 512
NORM_ROWS = 256
PART_ROWS = 256
FINISH_COLUMNS = 512
FINISH_LIMIT = 24
STORE_LIMIT = 24
PACKED = PART_ROWS * LOCAL // 2
BLOCK_ROWS = 64
MIB = 1 << 20


def lane_ids(rows):
    return lax.broadcasted_iota(jnp.int32, (rows, LANES), 1)


def local_kv(rank, head):
    return (rank * LOCAL + head) // GROUP - rank


def key_tile_start(rank):
    return rank // 2


def value_tile_start(rank):
    return jnp.where(rank == 0, 2, 3)


def key_offset(rank):
    return rank * HEAD_SIZE - key_tile_start(rank) * LANES


def value_offset(rank):
    return SPAN + rank * HEAD_SIZE - value_tile_start(rank) * LANES


def rotate(tile, cosine, sine):
    low = lane_ids(tile.shape[0]) % HEAD_SIZE < HEAD_SIZE // 2
    half = HEAD_SIZE // 2
    other = jnp.where(low, pltpu.roll(tile, LANES - half, 1), pltpu.roll(tile, half, 1))
    return tile * cosine + other * sine


def project_kernel(
    cache_len,
    group_len,
    page_map,
    hidden_hbm,
    gain,
    w_query_hbm,
    w_keyval_hbm,
    frequency,
    prior,
    queries_hbm,
    keyval_hbm,
    outgoing_hbm,
    own_hidden,
    queries,
    keyval,
    outgoing,
    live_rows,
    hidden,
    w_query,
    w_keyval,
    normed,
    mixed_q,
    mixed_kv,
    cosine,
    sine,
    semaphores,
    block_semaphores,
    store_semaphores,
    result_semaphores,
):
    cached, fresh = cache_len[0], group_len[0]
    rank = lax.axis_index("tp")
    total = hidden.shape[0]
    pieces = total // NORM_ROWS
    loads = [
        pltpu.make_async_copy(
            hidden_hbm.at[pl.ds(piece * NORM_ROWS, NORM_ROWS)],
            hidden.at[pl.ds(piece * NORM_ROWS, NORM_ROWS)],
            semaphores.at[piece],
        )
        for piece in range(pieces)
    ]
    weights = [
        pltpu.make_async_copy(w_keyval_hbm, w_keyval, semaphores.at[pieces]),
        pltpu.make_async_copy(w_query_hbm, w_query, semaphores.at[pieces + 1]),
    ]
    for copy in loads[:2] + weights + loads[2:]:
        copy.start()

    def prior_copy(block, slot):
        start = pl.multiple_of(block * BLOCK_ROWS, BLOCK_ROWS)
        return pltpu.make_async_copy(
            prior.at[pl.ds(start, BLOCK_ROWS)], outgoing.at[slot], block_semaphores.at[slot]
        )

    def block_store(slot):
        return pltpu.make_async_copy(
            outgoing.at[slot], outgoing_hbm.at[slot], store_semaphores.at[slot]
        )

    def send(block, carry):
        device = page_map[0, block]

        @pl.when(device & (TP - 1) == rank)
        def _():
            slot = device >> TP_BITS
            live = cached - block * BLOCK_ROWS
            live_rows[slot] = live

            @pl.when(live > 0)
            def _():
                prior_copy(block, slot).start()

        return carry

    prior_blocks = PRIOR_SLOTS // BLOCK_ROWS
    lax.fori_loop(0, prior_blocks, send, 0, unroll=8)
    for block in range(total // BLOCK_ROWS):
        device = page_map[0, prior_blocks + block]

        @pl.when(device & (TP - 1) == rank)
        def _():
            live_rows[device >> TP_BITS] = KEPT

    count = 32
    steps = lax.broadcasted_iota(jnp.int32, (count, LANES), 0)
    coarse = (steps * count + cached).astype(jnp.float32) * frequency[...]
    fine = steps.astype(jnp.float32) * frequency[...]
    coarse_cos, coarse_sin = jnp.cos(coarse), jnp.sin(coarse)
    fine_cos, fine_sin = jnp.cos(fine), jnp.sin(fine)
    low_half = lane_ids(count) % HEAD_SIZE < HEAD_SIZE // 2
    for step in range(total // count):
        here = pl.ds(step * count, count)
        far_cos, far_sin = coarse_cos[step : step + 1], coarse_sin[step : step + 1]
        cosine[here] = far_cos * fine_cos - far_sin * fine_sin
        both = far_sin * fine_cos + far_cos * fine_sin
        sine[here] = jnp.where(low_half, -both, both)

    def norm(piece):
        here = pl.ds(piece * NORM_ROWS, NORM_ROWS)
        value = hidden[here].astype(jnp.float32)
        scale = lax.rsqrt(jnp.mean(value * value, axis=-1, keepdims=True) + 1e-05)
        normed[here] = (value * scale * scale_row).astype(jnp.bfloat16)

    scale_row = gain[...].astype(jnp.float32).reshape(1, -1)
    lanes = lane_ids(PROJECT_ROWS)

    def mix(block):
        here = pl.ds(block * PROJECT_ROWS, PROJECT_ROWS)
        rows = normed[here]
        mixed_kv[here] = jnp.dot(rows, w_keyval[...], preferred_element_type=jnp.float32)
        mixed_q[here, :SPAN] = lax.dot_general(
            rows, w_query[...], (((1,), (1,)), ((), ())), preferred_element_type=jnp.float32
        )

    def turn(block):
        here = pl.ds(block * PROJECT_ROWS, PROJECT_ROWS)
        cos, sin = cosine[here], sine[here]
        for tile in range(WIDTH // LANES):
            columns = slice(tile * LANES, (tile + 1) * LANES)
            raw = mixed_kv[here, columns]
            if tile < 2:
                raw = rotate(raw, cos, sin)
            elif tile == 2:
                raw = jnp.where(lanes < HEAD_SIZE, rotate(raw, cos, sin), raw)
            keyval[here, columns] = raw.astype(jnp.bfloat16)
        for tile in range(3):
            raw = mixed_q[here, tile * LANES : (tile + 1) * LANES]
            turned = rotate(raw, cos, sin) * SCORE_SCALE
            for head in range(2 * tile, min(2 * tile + 2, LOCAL)):
                own = turned if head % 2 == 0 else pltpu.roll(turned, HEAD_SIZE, 1)
                queries[head, here] = own[:, :HEAD_SIZE].astype(jnp.bfloat16)

    def trim(slot, live, value):
        rows = lax.broadcasted_iota(jnp.int32, (BLOCK_ROWS, WIDTH), 0)
        outgoing[slot] = jnp.where(rows < live, value.astype(jnp.float32), 0.0).astype(jnp.bfloat16)

    def forward(slot, carry):
        live = live_rows[slot]

        @pl.when((live > 0) & (live < KEPT))
        def _():
            prior_copy(0, slot).wait()

        @pl.when((live > 0) & (live < BLOCK_ROWS))
        def _():
            trim(slot, live, outgoing[slot])

        @pl.when(live <= 0)
        def _():
            outgoing[slot] = jnp.zeros((BLOCK_ROWS, WIDTH), jnp.bfloat16)

        @pl.when(live < KEPT)
        def _():
            block_store(slot).start()

        return carry

    def result_stores(block):
        here = pl.ds(block * PROJECT_ROWS, PROJECT_ROWS)
        return [
            pltpu.make_async_copy(
                keyval.at[here], keyval_hbm.at[here], result_semaphores.at[0, block]
            ),
            pltpu.make_async_copy(
                queries.at[:, here], queries_hbm.at[:, here], result_semaphores.at[1, block]
            ),
        ]

    for piece in range(2):
        loads[piece].wait()
        norm(piece)
    for copy in weights:
        copy.wait()
    mix(0)
    for copy in loads[2:]:
        copy.wait()
    rows = own_hidden.shape[0]
    own_store = pltpu.make_async_copy(
        hidden.at[pl.ds(pl.multiple_of(rank * rows, rows), rows)],
        own_hidden,
        semaphores.at[pieces + 2],
    )
    own_store.start()
    norm(2)
    norm(3)
    lax.fori_loop(0, outgoing.shape[0], forward, 0, unroll=4)
    mix(1)
    turn(0)
    for copy in result_stores(0):
        copy.start()
    turn(1)
    for copy in result_stores(1):
        copy.start()
    for block in range(total // BLOCK_ROWS):
        device = page_map[0, prior_blocks + block]

        @pl.when(device & (TP - 1) == rank)
        def _():
            slot = device >> TP_BITS
            rows = keyval[pl.ds(block * BLOCK_ROWS, BLOCK_ROWS)]
            trim(slot, fresh - block * BLOCK_ROWS, rows)
            block_store(slot).start()

    own_store.wait()
    for slot in range(outgoing.shape[0]):
        block_store(slot).wait()
    for block in range(total // PROJECT_ROWS):
        for copy in result_stores(block):
            copy.wait()


def project(cache_len, group_len, page_map, hidden_in, norm_gain, w_query, w_keyval, prior):
    rows, model = hidden_in.shape
    half_size = HEAD_SIZE // 2
    frequency = 10000.0 ** (-(np.arange(half_size, dtype=np.float64) * 2.0 / HEAD_SIZE))
    frequency = jnp.asarray(np.tile(frequency, LANES // half_size)[None].astype(np.float32))
    count = page_map.shape[1] // TP
    scalar = pl.BlockSpec(memory_space=pltpu.SMEM)
    vector = pl.BlockSpec(memory_space=pltpu.VMEM)
    far = pl.BlockSpec(memory_space=pltpu.HBM)
    return pl.pallas_call(
        project_kernel,
        out_shape=(
            jax.ShapeDtypeStruct((LOCAL, rows, HEAD_SIZE), jnp.bfloat16),
            jax.ShapeDtypeStruct((rows, WIDTH), jnp.bfloat16),
            jax.ShapeDtypeStruct((count, BLOCK_ROWS, WIDTH), jnp.bfloat16),
            jax.ShapeDtypeStruct((rows // TP, model), jnp.bfloat16),
        ),
        in_specs=[scalar, scalar, scalar, far, vector, far, far, vector, far],
        out_specs=[far, far, far, far],
        scratch_shapes=[
            pltpu.VMEM((LOCAL, rows, HEAD_SIZE), jnp.bfloat16),
            pltpu.VMEM((rows, WIDTH), jnp.bfloat16),
            pltpu.VMEM((count, BLOCK_ROWS, WIDTH), jnp.bfloat16),
            pltpu.SMEM((count,), jnp.int32),
            pltpu.VMEM((rows, model), jnp.bfloat16),
            pltpu.VMEM((SPAN, model), jnp.bfloat16),
            pltpu.VMEM((model, WIDTH), jnp.bfloat16),
            pltpu.VMEM((rows, model), jnp.bfloat16),
            pltpu.VMEM((rows, 3 * LANES), jnp.float32),
            pltpu.VMEM((rows, WIDTH), jnp.float32),
            pltpu.VMEM((rows, LANES), jnp.float32),
            pltpu.VMEM((rows, LANES), jnp.float32),
            pltpu.SemaphoreType.DMA((rows // NORM_ROWS + 3,)),
            pltpu.SemaphoreType.DMA((count,)),
            pltpu.SemaphoreType.DMA((count,)),
            pltpu.SemaphoreType.DMA((2, rows // PROJECT_ROWS)),
        ],
        compiler_params=pltpu.CompilerParams(vmem_limit_bytes=58 * MIB),
        cost_estimate=pl.CostEstimate(
            flops=2 * rows * model * (SPAN + WIDTH), bytes_accessed=15 * MIB, transcendentals=0
        ),
        name="project",
    )(
        cache_len,
        group_len,
        page_map,
        hidden_in,
        norm_gain,
        w_query.T,
        w_keyval,
        frequency,
        prior,
    )


def attend_kernel(
    cache_len,
    group_len,
    queries_hbm,
    prior,
    fresh_rows,
    *rest,
):
    outs = rest[:TP]
    heads_out, queries, raw_keys, raw_values, keys, values, top, total, semaphores = rest[TP:]
    cached, fresh, rank = cache_len[0], group_len[0], lax.axis_index("tp")
    key_start = pl.multiple_of(key_tile_start(rank) * LANES, LANES)
    value_start = pl.multiple_of(value_tile_start(rank) * LANES, LANES)
    key_shift, value_shift = key_offset(rank), value_offset(rank)
    prior_chunks = (cached + KEY_ROWS - 1) // KEY_ROWS
    blocks = (fresh + QUERY_ROWS - 1) // QUERY_ROWS
    chunk_limit = PRIOR_SLOTS // KEY_ROWS

    def copies(chunk):
        into = pl.ds(chunk * KEY_ROWS, KEY_ROWS)
        return (
            pltpu.make_async_copy(
                prior.at[into, pl.ds(key_start, WINDOW)],
                raw_keys.at[into],
                semaphores.at[0, chunk],
            ),
            pltpu.make_async_copy(
                prior.at[into, pl.ds(value_start, WINDOW)],
                raw_values.at[into],
                semaphores.at[1, chunk],
            ),
        )

    into = pl.ds(PRIOR_SLOTS, NEW_TOKEN_SLOTS)
    fresh_copies = (
        pltpu.make_async_copy(
            fresh_rows.at[:, pl.ds(key_start, WINDOW)],
            raw_keys.at[into],
            semaphores.at[0, chunk_limit],
        ),
        pltpu.make_async_copy(
            fresh_rows.at[:, pl.ds(value_start, WINDOW)],
            raw_values.at[into],
            semaphores.at[1, chunk_limit],
        ),
    )
    fresh_copies += (
        pltpu.make_async_copy(queries_hbm, queries, semaphores.at[0, chunk_limit + 1]),
    )
    for copy in fresh_copies:
        copy.start()
    for chunk in range(chunk_limit):

        @pl.when(chunk < prior_chunks)
        def _():
            for copy in copies(chunk):
                copy.start()

    def prepare(start, live):
        here = pl.ds(start, PREPARE_ROWS)
        lanes = lane_ids(PREPARE_ROWS)
        alive = lax.broadcasted_iota(jnp.int32, (PREPARE_ROWS, LANES), 0) < live
        raw = raw_keys[here].astype(jnp.float32)
        low, high = raw[:, :LANES], raw[:, LANES:]
        spare = raw_keys[0:8].astype(jnp.float32)[0:1]
        low = jnp.where(alive, low, spare[:, :LANES])
        high = jnp.where(alive, high, spare[:, LANES:])
        joined = jnp.where(
            lanes < HEAD_SIZE, pltpu.roll(low, HEAD_SIZE, 1), pltpu.roll(high, HEAD_SIZE, 1)
        )
        pair = jnp.where(key_shift == 0, low, joined)
        keys[:, here] = pair.T.astype(jnp.bfloat16)
        raw = raw_values[here].astype(jnp.float32)
        low, high = raw[:, :LANES], raw[:, LANES:]
        low_turned, high_turned = pltpu.roll(low, HEAD_SIZE, 1), pltpu.roll(high, HEAD_SIZE, 1)
        one = jnp.where(
            value_shift == 0, low, jnp.where(value_shift == HEAD_SIZE, low_turned, high)
        )
        two = jnp.where(
            value_shift == 0, low_turned, jnp.where(value_shift == HEAD_SIZE, high, high_turned)
        )
        for slot, own in enumerate((one, two)):
            own = jnp.where(alive, jnp.where(lanes < HEAD_SIZE, own, 1.0), 0.0)
            values[slot, here] = own.astype(jnp.bfloat16)

    def score(span, head, start, rows):
        which = local_kv(rank, head)
        return jnp.dot(
            queries[head, span],
            keys[pl.ds(pl.multiple_of(which * HEAD_SIZE, HEAD_SIZE), HEAD_SIZE), pl.ds(start, rows)],
            preferred_element_type=jnp.float32,
        )

    def blend(span, head, start, rows, scores, masked):
        if masked:
            row = lax.broadcasted_iota(jnp.int32, scores.shape, 0)
            column = lax.broadcasted_iota(jnp.int32, scores.shape, 1)
            scores = jnp.where(column <= row, scores, -1e30)
        before = top[head, span]
        after = jnp.maximum(before, jnp.max(scores, axis=-1, keepdims=True))
        rescale = jnp.exp2(before - after)
        chances = jnp.exp2(scores - jnp.tile(after, (1, rows // LANES))).astype(jnp.bfloat16)
        top[head, span] = after
        total[head, span] = total[head, span] * rescale + jnp.dot(
            chances,
            values[local_kv(rank, head), pl.ds(start, rows)],
            preferred_element_type=jnp.float32,
        )

    def absorb(span, start, rows, masked=False):
        pieces = [
            (head, slice(begin, begin + QUERY_ROWS))
            for head in range(LOCAL)
            for begin in range(span.start, span.stop, QUERY_ROWS)
        ]
        pending = score(pieces[0][1], pieces[0][0], start, rows)
        for index, (head, piece) in enumerate(pieces):
            following = None
            if index + 1 < len(pieces):
                following = score(pieces[index + 1][1], pieces[index + 1][0], start, rows)
            blend(piece, head, start, rows, pending, masked)
            pending = following

    lower, upper = slice(0, QUERY_ROWS), slice(QUERY_ROWS, 2 * QUERY_ROWS)
    everything = slice(0, 2 * QUERY_ROWS)
    top[...] = jnp.full_like(top, -1e30)
    total[...] = jnp.zeros_like(total)
    for copy in fresh_copies:
        copy.wait()

    def prepare_fresh(step, inner):
        start = pl.multiple_of(PRIOR_SLOTS + step * PREPARE_ROWS, PREPARE_ROWS)
        prepare(start, PREPARE_ROWS)
        return inner

    lax.fori_loop(0, NEW_TOKEN_SLOTS // PREPARE_ROWS, prepare_fresh, 0)
    absorb(lower, PRIOR_SLOTS, QUERY_ROWS, True)

    @pl.when(blocks > 1)
    def _():
        absorb(upper, PRIOR_SLOTS, QUERY_ROWS)
        absorb(upper, PRIOR_SLOTS + QUERY_ROWS, QUERY_ROWS, True)

    def cache(step, carry):
        start = pl.multiple_of(step * KEY_ROWS, KEY_ROWS)
        for copy in copies(step):
            copy.wait()

        def each(part, most):
            here = pl.multiple_of(start + part * PREPARE_ROWS, PREPARE_ROWS)
            prepare(here, cached - here)
            return most

        lax.fori_loop(0, KEY_ROWS // PREPARE_ROWS, each, 0)

        @pl.when(blocks > 1)
        def _():
            absorb(everything, start, KEY_ROWS)

        @pl.when(blocks <= 1)
        def _():
            absorb(lower, start, KEY_ROWS)

        return carry

    lax.fori_loop(0, prior_chunks, cache, 0)

    def query_block(block, carry):
        here = pl.ds(pl.multiple_of(block * QUERY_ROWS, QUERY_ROWS), QUERY_ROWS)
        lanes = lane_ids(QUERY_ROWS)
        odd = rank % 2 == 1
        plain, turned = [], []
        for head in range(LOCAL):
            sums = total[head, here]
            swapped = pltpu.roll(sums, HEAD_SIZE, 1)
            plain.append(sums / swapped)
            turned.append(swapped / sums)
        even_pairs = [jnp.where(lanes < HEAD_SIZE, plain[i], turned[i + 1]) for i in (0, 2)]
        odd_pairs = [jnp.where(lanes < HEAD_SIZE, plain[i], turned[i + 1]) for i in (1, 3)]
        single = jnp.where(odd, plain[0], plain[4])
        single_turned = jnp.where(odd, turned[0], turned[4])
        near = (lane_ids(LANES) < HEAD_SIZE) != odd
        for part in range(QUERY_ROWS // PART_ROWS):
            slot = (block * (QUERY_ROWS // PART_ROWS) + part + TP - rank) & (TP - 1)
            rows = slice(part * PART_ROWS, (part + 1) * PART_ROWS)
            for tile in range(2):
                pair = jnp.where(odd, odd_pairs[tile][rows], even_pairs[tile][rows])
                heads_out[slot, tile * PART_ROWS : (tile + 1) * PART_ROWS] = pair.astype(
                    jnp.bfloat16
                )
            begin = part * PART_ROWS
            above, below = slice(begin, begin + LANES), slice(begin + LANES, begin + PART_ROWS)
            packed = jnp.where(
                odd,
                jnp.where(near, single_turned[above], single[below]),
                jnp.where(near, single[above], single_turned[below]),
            )
            heads_out[slot, 2 * PART_ROWS :] = packed.astype(jnp.bfloat16)
        return carry

    lax.fori_loop(0, blocks, query_block, 0)

    def idle(part, carry):
        heads_out[(part + TP - rank) & (TP - 1)] = jnp.zeros((PACKED, LANES), jnp.bfloat16)
        return carry

    parts = QUERY_ROWS // PART_ROWS
    lax.fori_loop(blocks * parts, QUERY_BLOCKS * parts, idle, 0)
    for shift, out in enumerate(outs):
        out[...] = heads_out[shift]


def attend(cache_len, group_len, queries, prior, fresh_rows):
    context = PRIOR_SLOTS + NEW_TOKEN_SLOTS
    vector = pl.BlockSpec(memory_space=pltpu.VMEM)
    return pl.pallas_call(
        attend_kernel,
        out_shape=[jax.ShapeDtypeStruct((PACKED, LANES), jnp.bfloat16)] * TP,
        in_specs=[
            pl.BlockSpec(memory_space=pltpu.SMEM),
            pl.BlockSpec(memory_space=pltpu.SMEM),
            pl.BlockSpec(memory_space=pl.ANY),
            pl.BlockSpec(memory_space=pltpu.HBM),
            pl.BlockSpec(memory_space=pl.ANY),
        ],
        out_specs=[vector] * TP,
        scratch_shapes=[
            pltpu.VMEM((TP, PACKED, LANES), jnp.bfloat16),
            pltpu.VMEM(queries.shape, queries.dtype),
            pltpu.VMEM((context, WINDOW), jnp.bfloat16),
            pltpu.VMEM((context, WINDOW), jnp.bfloat16),
            pltpu.VMEM((LANES, context), jnp.bfloat16),
            pltpu.VMEM((2, context, LANES), jnp.bfloat16),
            pltpu.VMEM((LOCAL, NEW_TOKEN_SLOTS, LANES), jnp.float32),
            pltpu.VMEM((LOCAL, NEW_TOKEN_SLOTS, LANES), jnp.float32),
            pltpu.SemaphoreType.DMA((2, PRIOR_SLOTS // KEY_ROWS + 2)),
        ],
        compiler_params=pltpu.CompilerParams(vmem_limit_bytes=56 * MIB),
        cost_estimate=pl.CostEstimate(
            flops=4 * 5120 * 7680 * 256, bytes_accessed=12 * MIB, transcendentals=5120 * 7680
        ),
        name="attend",
    )(cache_len, group_len, queries, prior, fresh_rows)


def store_kernel(received, w_out, decode, w_near, semaphores):
    copies = (
        pltpu.make_async_copy(w_out, w_near, semaphores.at[0]),
        pltpu.make_async_copy(received, decode, semaphores.at[1]),
    )
    for copy in copies:
        copy.start()
    for copy in copies:
        copy.wait()


def store_blocks(received, w_out):
    vector = pl.BlockSpec(memory_space=pltpu.VMEM)
    far = pl.BlockSpec(memory_space=pltpu.HBM)
    return pl.pallas_call(
        store_kernel,
        out_shape=(
            jax.ShapeDtypeStruct(received.shape, received.dtype),
            jax.ShapeDtypeStruct(w_out.shape, w_out.dtype),
        ),
        in_specs=[vector, far],
        out_specs=[far, vector],
        scratch_shapes=[pltpu.SemaphoreType.DMA((2,))],
        compiler_params=pltpu.CompilerParams(vmem_limit_bytes=STORE_LIMIT * MIB),
        cost_estimate=pl.CostEstimate(flops=0, bytes_accessed=12 * MIB, transcendentals=0),
        name="store_blocks",
    )(received, w_out)


def finish_kernel(group_len, own, *rest):
    travelled = rest[: TP - 1]
    w_out, hidden, result, heads, joined = rest[TP - 1 :]
    rank, fresh = lax.axis_index("tp"), group_len[0]
    rows = result.shape[0]
    wide = FINISH_COLUMNS
    steps = result.shape[1] // wide
    for shift, source in enumerate((own,) + tuple(travelled)):
        heads[(rank + TP - shift) & (TP - 1)] = source[...]
    low = lane_ids(LANES) < HEAD_SIZE
    for pair in range(2):
        first, second = heads.at[2 * pair], heads.at[2 * pair + 1]
        for tile in range(2):
            source = slice(tile * PART_ROWS, (tile + 1) * PART_ROWS)
            columns = (5 * pair + tile) * LANES
            joined[:, columns : columns + LANES] = first[source]
            joined[:, columns + 3 * LANES : columns + 4 * LANES] = second[source]
        one = first[2 * PART_ROWS :].astype(jnp.float32)
        two = second[2 * PART_ROWS :].astype(jnp.float32)
        columns = (5 * pair + 2) * LANES
        joined[:LANES, columns : columns + LANES] = jnp.where(low, one, two).astype(jnp.bfloat16)
        one, two = pltpu.roll(one, HEAD_SIZE, 1), pltpu.roll(two, HEAD_SIZE, 1)
        joined[LANES:, columns : columns + LANES] = jnp.where(low, one, two).astype(jnp.bfloat16)
    alive = lax.broadcasted_iota(jnp.int32, (rows, wide), 0) + rank * rows < fresh
    for step in range(steps):
        columns = slice(step * wide, (step + 1) * wide)
        mixed = jnp.dot(joined[...], w_out[:, columns], preferred_element_type=jnp.float32)
        value = hidden[:, columns].astype(jnp.float32) + mixed
        result[:, columns] = jnp.where(alive, value, 0.0).astype(jnp.bfloat16)


def finish(group_len, heads, w_out, hidden):
    model = w_out.shape[1]
    vector = pl.BlockSpec(memory_space=pltpu.VMEM)
    return pl.pallas_call(
        finish_kernel,
        out_shape=jax.ShapeDtypeStruct((PART_ROWS, model), jnp.bfloat16),
        in_specs=[pl.BlockSpec(memory_space=pltpu.SMEM)] + [vector] * (TP + 2),
        out_specs=vector,
        scratch_shapes=[
            pltpu.VMEM((TP, PACKED, LANES), jnp.bfloat16),
            pltpu.VMEM((PART_ROWS, w_out.shape[0]), jnp.bfloat16),
        ],
        compiler_params=pltpu.CompilerParams(vmem_limit_bytes=FINISH_LIMIT * MIB),
        cost_estimate=pl.CostEstimate(
            flops=2 * PART_ROWS * w_out.shape[0] * model,
            bytes_accessed=8 * MIB,
            transcendentals=0,
        ),
        name="finish",
    )(group_len, *heads, w_out, hidden)


def shards(
    hidden_in,
    norm_gain,
    w_query,
    key_value_weight,
    w_out,
    prior_cache,
    cache_len,
    group_len,
    page_map,
):
    prior = prior_cache[0]
    queries, keyval, outgoing, own_hidden = project(
        cache_len, group_len, page_map, hidden_in, norm_gain, w_query, key_value_weight, prior
    )
    outgoing, queries = lax.optimization_barrier((outgoing, queries))
    received = lax.all_to_all(outgoing, "req", split_axis=0, concat_axis=0, tiled=True)
    attended = attend(cache_len, group_len, queries, prior, keyval)
    attended, received = lax.optimization_barrier((attended, received))
    heads = [attended[0]]
    for shift in range(1, TP):
        pairs = [(source, (source + shift) % TP) for source in range(TP)]
        heads.append(lax.ppermute(attended[shift], "tp", pairs))
    decode_kv, w_near = store_blocks(received, w_out)
    hidden_out = finish(group_len, heads, w_near, own_hidden)
    return (hidden_out, decode_kv[None])


def solution(mesh):
    placed = (
        P("req", None),
        P(),
        P(None, "tp"),
        P(),
        P(),
        P("req", None, None),
        P("req"),
        P("req"),
        P("req", None),
    )
    return jax.shard_map(
        shards,
        mesh=mesh,
        in_specs=placed,
        out_specs=(P(("req", "tp"), None), P(("req", "tp"), None, None, None)),
        check_vma=False,
    )
```
